512 devices in a mesh: cols: 128 (over x, z, core), trc: 4 (over y).
Axes of the slice: x: 4, y: 4, z: 16, core: 2. Of those that a mesh axis runs over, the one named last changes fastest.
Arguments:
- tracers: float32 [8, 137, 32768], P('trc', None, 'cols'), may hold values from 0.05 to 5
- dep_frac: float32 [2, 32768], P(None, 'cols'), may hold values from 0 to 1
- vert_frac: float32 [137, 32768], P(None, 'cols'), may hold values from 0 to 1
- vert_base: int32 [137, 32768], P(None, 'cols'), may hold values from 0 to 133, as said below
- dep_blocks: int32 [128, 5, 1], P('cols'), may hold values from 0 to 1, as said below
- dep_slot: int32 [32768], P('cols'), may hold values from 0 to 4, as said below
- dep_off: int32 [32768], P('cols'), may hold values from 0 to 76, as said below
- remap_share: float32 [32768], P('cols'), may hold values from 0.1 to 0.5
- remap_target: int32 [32768], P('cols'), may hold values from 0 to 32767, as said below
- species_share: float32 [8], P('trc'), may hold values from 0.25 to 4
Outputs:
- advected: float32 [8, 137, 32768], P('trc', None, 'cols')
The draws below stay inside these ranges and needn't reach their ends.
Inputs may be any that keep to these rules, and one draw needn't show every extreme that they name: `dep_blocks`: for each tile and offset the entries are distinct block numbers of that tile. `dep_slot`: names an entry of its tile's list. `dep_off`: equals 16 r + s with r at most 4 and s at most 12, so the 4 x 4 stencil stays inside the block. Levels vert_base to vert_base + 3 exist, and vert_base[l, c] lies within l - 3 to l + 1. `remap_target`: at most 4 columns of one tile have targets on any one tile, and some tile receives exactly 4 from every tile.
All inputs are finite; a program needn't handle non-finite values.
Results may differ from the reference program's by a relative error of at most 0.0001.
Values sent between devices are 32-bit elements; how exact they have to be, the bound alone decides.
No kernel may reach another device: no remote copies, remote signals or barrier semaphores. Data moves between devices by JAX's collectives and lax.ppermute only.
A program may use at most 64 MiB of HBM per device.

```python
import math
import jax
import jax.numpy as jnp

LEVELS = 137
TRACERS = 8
BLOCK = 128
BLOCKS = 2
REACH = 2
ASKED = 1
STEPS = 2
COLUMNS = 32768
N_COLS = 128


def fetch_lists(key):
    folded = jax.random.fold_in(key, 11)
    subkeys = jax.random.split(folded, 4)
    offsets_all = 2 * REACH + 1
    tile_cols = BLOCKS * BLOCK
    total_cols = tile_cols * N_COLS
    counts = jax.random.randint(subkeys[0], (N_COLS, offsets_all), 1, ASKED + 1)
    full_at = jax.random.randint(subkeys[1], (N_COLS,), 0, offsets_all)
    counts = jnp.where(jnp.arange(offsets_all)[None, :] == full_at[:, None], ASKED, counts)
    scores = jax.random.randint(subkeys[2], (N_COLS, offsets_all, BLOCKS), 0, 1 << 20) * BLOCKS + jnp.arange(BLOCKS)[None, None, :]
    ordering = jnp.argsort(scores, axis=-1)[:, :, :ASKED]
    in_use = jnp.arange(ASKED)[None, None, :] < counts[:, :, None]
    blocks_list = jnp.where(in_use, ordering, -1).astype(jnp.int32)
    flat_use = in_use.reshape(N_COLS, offsets_all * ASKED)
    position = jnp.arange(offsets_all * ASKED)[None, :]
    ranked = jnp.argsort(jnp.where(flat_use, position, offsets_all * ASKED + position), axis=1)
    reader = jnp.arange(total_cols) // tile_cols
    live_count = jnp.sum(counts, axis=1)
    chosen_rank = jax.random.randint(subkeys[3], (total_cols,), 0, live_count[reader])
    slots = ranked[reader, chosen_rank].astype(jnp.int32)
    return (blocks_list, slots)


def draw_dep_blocks(key, part):
    return fetch_lists(key)[0]


def draw_dep_slot(key, part):
    return fetch_lists(key)[1]


def draw_dep_off(key, part):
    subkeys = jax.random.split(jax.random.fold_in(key, 23), 2)
    total_cols = BLOCKS * BLOCK * N_COLS
    patch_rows = jax.random.randint(subkeys[0], (total_cols,), 0, BLOCK // 16 - 3)
    patch_places = jax.random.randint(subkeys[1], (total_cols,), 0, 13)
    return (16 * patch_rows + patch_places).astype(jnp.int32)


def draw_vert_base(key, part):
    total_cols = BLOCKS * BLOCK * N_COLS
    jitter = jax.random.randint(jax.random.fold_in(key, 37), (LEVELS, total_cols), -2, 3)
    level_index = jnp.arange(LEVELS)[:, None]
    return jnp.clip(level_index - 1 + jitter, 0, LEVELS - 4).astype(jnp.int32)


def draw_remap_target(key, part):
    subkeys = jax.random.split(jax.random.fold_in(key, 53), 4)
    tile_cols = BLOCKS * BLOCK
    per_owner = 2 * tile_cols // N_COLS
    slot_count = N_COLS * per_owner
    hot_owner = jax.random.randint(subkeys[0], (), 0, N_COLS)
    spread = (1 << 30) // slot_count - 2
    raw_score = jax.random.randint(subkeys[1], (N_COLS, slot_count), 0, spread)
    slot_ids = jnp.arange(slot_count)[None, :]
    slot_score = jnp.where(slot_ids // per_owner == hot_owner, slot_ids, slot_count + raw_score * slot_count + slot_ids)
    chosen = jnp.argsort(slot_score, axis=1)[:, :tile_cols]
    shuffle_score = jax.random.randint(subkeys[2], (N_COLS, tile_cols), 0, spread) * tile_cols + jnp.arange(tile_cols)[None, :]
    ordering = jnp.argsort(shuffle_score, axis=1)
    placed = jnp.take_along_axis(chosen, ordering, axis=1)
    owner_tile = placed // per_owner
    cell_index = jax.random.randint(subkeys[3], (N_COLS, tile_cols), 0, tile_cols)
    return (owner_tile * tile_cols + cell_index).reshape(N_COLS * tile_cols).astype(jnp.int32)


def levels(rng, extent, cuts, low, top_value):
    def one(dim, blocks):
        draws = jax.random.uniform(jax.random.fold_in(jax.random.fold_in(rng, 6), dim), (blocks,), jnp.float32, low / len(cuts), top_value / len(cuts))
        return jnp.repeat(jnp.exp(draws), extent[dim] // blocks).reshape((-1,) + (1,) * (len(extent) - dim - 1))

    factor_of = one(*cuts[0])
    for cut in cuts[1:]:
        factor_of = factor_of * one(*cut)
    return factor_of


def setup_inputs(seed: int = 0) -> dict:
    streams_of = jax.random.split(jax.random.key(seed), 11)
    tracers = jnp.clip(jnp.exp(math.log(5.0) - 4.6051702 * jax.random.uniform(streams_of[0], (TRACERS, LEVELS, COLUMNS), jnp.float32) ** levels(streams_of[0], (TRACERS, LEVELS, COLUMNS), ((0, 4), (2, 128)), -0.2, 0.2)), 0.05, 5.0)
    dep_frac = jnp.clip(1.0 * jax.random.uniform(streams_of[1], (2, COLUMNS), jnp.float32) ** levels(streams_of[1], (2, COLUMNS), ((1, 128),), -0.2, 0.2), 0.0, 1.0)
    vert_frac = jnp.clip(1.0 * jax.random.uniform(streams_of[2], (LEVELS, COLUMNS), jnp.float32) ** levels(streams_of[2], (LEVELS, COLUMNS), ((1, 128),), -0.2, 0.2), 0.0, 1.0)
    vert_base = draw_vert_base(jax.random.fold_in(streams_of[10], 71), 0)
    dep_blocks = draw_dep_blocks(jax.random.fold_in(streams_of[10], 71), 0)
    dep_slot = draw_dep_slot(jax.random.fold_in(streams_of[10], 71), 0)
    dep_off = draw_dep_off(jax.random.fold_in(streams_of[10], 71), 0)
    remap_share = jnp.clip(0.1 + 0.4 * jax.random.uniform(streams_of[7], (COLUMNS,), jnp.float32) ** levels(streams_of[7], (COLUMNS,), ((0, 128),), -0.2, 0.2), 0.1, 0.5)
    remap_target = draw_remap_target(jax.random.fold_in(streams_of[10], 71), 0)
    species_share = jnp.clip(jnp.exp(math.log(4.0) - 2.7725887 * jax.random.uniform(streams_of[9], (TRACERS,), jnp.float32) ** levels(streams_of[9], (TRACERS,), ((0, 4),), -0.2, 0.2)), 0.25, 4.0)
    return {"tracers": tracers, "dep_frac": dep_frac, "vert_frac": vert_frac, "vert_base": vert_base, "dep_blocks": dep_blocks, "dep_slot": dep_slot, "dep_off": dep_off, "remap_share": remap_share, "remap_target": remap_target, "species_share": species_share}


def cubic_weights(fraction):
    return (-fraction * (fraction - 1.0) * (fraction - 2.0) / 6.0,
            (fraction + 1.0) * (fraction - 1.0) * (fraction - 2.0) / 2.0,
            -(fraction + 1.0) * fraction * (fraction - 2.0) / 2.0,
            (fraction + 1.0) * fraction * (fraction - 1.0) / 6.0)


def interpolate(source, first_col, lon_weights, lat_weights, vert_weights, vert_base):
    horizontal = None
    for stencil_row in range(4):
        for stencil_place in range(4):
            picked = jnp.take(source, first_col + 16 * stencil_row + stencil_place, axis=2)
            contrib = (lat_weights[stencil_row] * lon_weights[stencil_place])[None, None, :] * picked
            horizontal = contrib if horizontal is None else horizontal + contrib
    interpolated = None
    for vert_tap in range(4):
        picked = jnp.take_along_axis(horizontal, (vert_base + vert_tap)[None, :, :], axis=1)
        contrib = vert_weights[vert_tap][None, :, :] * picked
        interpolated = contrib if interpolated is None else interpolated + contrib
    return interpolated


def reference(tracers, dep_frac, vert_frac, vert_base, dep_blocks, dep_slot, dep_off, remap_share, remap_target, species_share):
    columns_all = tracers.shape[2]
    tile_cols = columns_all // N_COLS
    reader = jnp.arange(columns_all, dtype=jnp.int32) // tile_cols
    entry = dep_slot // ASKED
    within = dep_slot % ASKED
    chosen_block = dep_blocks[reader, entry, within]
    owner_tile = (reader + entry - REACH) % N_COLS
    first_col = (owner_tile * tile_cols + chosen_block * BLOCK + dep_off).astype(jnp.int32)
    lon_weights = cubic_weights(dep_frac[0])
    lat_weights = cubic_weights(dep_frac[1])
    vert_weights = cubic_weights(vert_frac)
    share_norm = species_share / jnp.sum(species_share)
    current = tracers
    for step_index in range(STEPS):
        interpolated = interpolate(current, first_col, lon_weights, lat_weights, vert_weights, vert_base)
        deficit = jnp.sum(jnp.minimum(interpolated, 0.0), axis=0)
        fixed = jnp.maximum(interpolated, 0.0) + share_norm[:, None, None] * deficit[None, :, :]
        deposit = jnp.zeros_like(fixed).at[:, :, remap_target].add(remap_share[None, None, :] * fixed)
        current = (1.0 - remap_share)[None, None, :] * fixed + deposit
    return current
```

```python
import functools

import jax
import jax.numpy as jnp
from jax import lax
from jax.experimental import pallas as pl
from jax.experimental.pallas import tpu as pltpu
from jax.sharding import PartitionSpec as P

BLOCK = 128
REACH = 2
STEPS = 2
LEVELS = 137
TILE = 256
TILES = 128
SLOTS = 4
OFFSETS = 2 * REACH + 1
SOURCE = OFFSETS * BLOCK
ROWS = 9
PAD = 144
VMEM = pl.BlockSpec(memory_space=pltpu.VMEM)
SMEM = pl.BlockSpec(memory_space=pltpu.SMEM)
F32 = jnp.float32
BF16 = jnp.bfloat16


def from_behind(value, axis, steps):
    count = lax.axis_size(axis)
    pairs = [(source, (source + steps) % count) for source in range(count)]
    return lax.ppermute(value, axis, pairs)


def cubic_weights(fraction):
    return (
        -fraction * (fraction - 1.0) * (fraction - 2.0) / 6.0,
        (fraction + 1.0) * (fraction - 1.0) * (fraction - 2.0) / 2.0,
        -(fraction + 1.0) * fraction * (fraction - 2.0) / 2.0,
        (fraction + 1.0) * fraction * (fraction - 1.0) / 6.0,
    )


def three_parts(value):
    high = value.astype(BF16)
    rest = value - high.astype(F32)
    middle = rest.astype(BF16)
    low = (rest - middle.astype(F32)).astype(BF16)
    return high, middle, low


def pick(index, choices):
    value = jnp.where(index == 1, choices[1], choices[0])
    value = jnp.where(index == 2, choices[2], value)
    return jnp.where(index == 3, choices[3], value)


def prepare_kernel(frac_ref, slot_ref, off_ref, target_ref, weight_ref, send_ref, cell_ref):
    lon = cubic_weights(frac_ref[0:1, :])
    lat = cubic_weights(frac_ref[1:2, :])
    first = slot_ref[...].reshape(1, TILE) * BLOCK + off_ref[...].reshape(1, TILE)
    for part in range(OFFSETS):
        row = lax.broadcasted_iota(jnp.int32, (BLOCK, TILE), 0) + part * BLOCK
        away = row - first
        place = away & 15
        inside = (away >= 0) & (away < 64) & (place < 4)
        weight = pick(away >> 4, lat) * pick(place, lon)
        weight_ref[part * BLOCK : (part + 1) * BLOCK, :] = jnp.where(inside, weight, 0.0)
    target = target_ref[...].reshape(1, TILE)
    owner = target >> 8
    hit = lax.broadcasted_iota(jnp.int32, (TILES, TILE), 0) == owner
    earlier = lax.broadcasted_iota(jnp.int32, (TILE, TILE), 0) < lax.broadcasted_iota(
        jnp.int32, (TILE, TILE), 1
    )
    one_hot = jnp.where(hit, 1.0, 0.0)
    rank = jnp.dot(
        one_hot.astype(BF16),
        jnp.where(earlier, 1.0, 0.0).astype(BF16),
        preferred_element_type=F32,
    )
    for slot in range(SLOTS):
        chosen = jnp.where(rank == slot, one_hot, 0.0)
        send_ref[slot * TILES : (slot + 1) * TILES, :] = chosen.astype(BF16)
    cell_ref[...] = ((target & (TILE - 1)) + 1).astype(F32)


def interpolate_kernel(
    blocks_ref, share_ref, s0, s1, s2, s3, s4, weight_ref, frac_ref, base_ref, out_ref, neg_ref, pad_ref
):
    weight = weight_ref[...]
    for n in range(2):
        pieces = []
        for part, source in enumerate((s0, s1, s2, s3, s4)):
            start = pl.multiple_of(blocks_ref[0, part, 0] * BLOCK, BLOCK)
            pieces.append(source[n, :, pl.ds(start, BLOCK)])
        joined = jnp.concatenate(pieces, axis=1)
        pad_ref[n, 0:8, :] = jnp.zeros((8, TILE), F32)
        pad_ref[n, 144:152, :] = jnp.zeros((8, TILE), F32)
        pad_ref[n, 8 : 8 + LEVELS, :] = jnp.dot(
            joined, weight, precision=lax.Precision.HIGHEST, preferred_element_type=F32
        )
    vert = cubic_weights(frac_ref[...])
    level = lax.broadcasted_iota(jnp.int32, (LEVELS, TILE), 0)
    away = base_ref[...] - level
    same = [away == shift for shift in range(-3, 2)]
    total = [jnp.zeros((LEVELS, TILE), F32), jnp.zeros((LEVELS, TILE), F32)]
    for delta in range(-3, 5):
        factor = jnp.zeros((LEVELS, TILE), F32)
        for tap in range(4):
            if -3 <= delta - tap <= 1:
                factor = jnp.where(same[delta - tap + 3], vert[tap], factor)
        for n in range(2):
            total[n] = total[n] + factor * pad_ref[n, 8 + delta : 8 + delta + LEVELS, :]
    out_ref[0] = total[0]
    out_ref[1] = total[1]
    neg_ref[136:PAD, :] = jnp.full((8, TILE), share_ref[0] + share_ref[1], F32)
    neg_ref[0:LEVELS, :] = jnp.minimum(total[0], 0.0) + jnp.minimum(total[1], 0.0)


def send_kernel(
    share_ref, mixed_ref, d0, d1, d2, d3, remap_ref, send_ref, cell_ref, kept_ref, out_ref, x_ref
):
    all_parts = d0[...] + d1[...] + d2[...] + d3[...]
    deficit = all_parts[0:LEVELS, :]
    whole = all_parts[LEVELS : LEVELS + 1, :]
    remap = remap_ref[...].reshape(1, TILE)
    x_ref[256:384, :] = jnp.zeros((128, TILE), F32)
    for n in range(2):
        fixed = jnp.maximum(mixed_ref[n], 0.0) + (share_ref[n] / whole) * deficit
        kept_ref[n] = (1.0 - remap) * fixed
        moved = remap * fixed
        x_ref[n * 128 : n * 128 + 128, :] = moved[0:128, :]
        x_ref[256 + 16 * n : 256 + 16 * n + 9, :] = moved[128:LEVELS, :]
    x_ref[265:266, :] = cell_ref[...]
    send = send_ref[...]
    dims = (((1,), (1,)), ((), ()))
    result = None
    for piece in three_parts(x_ref[...]):
        term = lax.dot_general(send, piece, dims, preferred_element_type=F32)
        result = term if result is None else result + term
    rest = None
    for slot in range(SLOTS):
        rows = result[slot * TILES : (slot + 1) * TILES, :]
        for n in range(2):
            out_ref[pl.ds(2 * slot + n, TILES, stride=ROWS), :] = rows[:, n * 128 : n * 128 + 128]
        tail = rows[:, 256:384]
        if slot:
            tail = pltpu.roll(tail, 32 * slot, axis=1)
        rest = tail if rest is None else rest + tail
    out_ref[pl.ds(8, TILES, stride=ROWS), :] = rest


def land_kernel(kept_ref, got_ref, out_ref):
    rest = got_ref[pl.ds(8, TILES, stride=ROWS), :].T
    column = (lax.broadcasted_iota(jnp.int32, (TILE, TILES), 0) + 1).astype(F32)
    sums = [None, None]
    tails = [None, None]
    for slot in range(SLOTS):
        cell = rest[32 * slot + 9 : 32 * slot + 10, :]
        landing = jnp.where(column == cell, 1.0, 0.0).astype(BF16)
        for n in range(2):
            for piece in three_parts(got_ref[pl.ds(2 * slot + n, TILES, stride=ROWS), :]):
                term = jnp.dot(landing, piece, preferred_element_type=F32)
                sums[n] = term if sums[n] is None else sums[n] + term
            tail = rest[32 * slot + 16 * n : 32 * slot + 16 * n + 16, :]
            for piece in three_parts(tail):
                term = lax.dot_general(
                    piece, landing, (((1,), (1,)), ((), ())), preferred_element_type=F32
                )
                tails[n] = term if tails[n] is None else tails[n] + term
    for n in range(2):
        out_ref[n, 0:128, :] = kept_ref[n, 0:128, :] + sums[n].T
        out_ref[n, 128:LEVELS, :] = kept_ref[n, 128:LEVELS, :] + tails[n][0 : LEVELS - 128, :]


def cost(flops, moved):
    return pl.CostEstimate(flops=flops, bytes_accessed=moved, transcendentals=0)


def shards(
    tracers,
    dep_frac,
    vert_frac,
    vert_base,
    dep_blocks,
    dep_slot,
    dep_off,
    remap_share,
    remap_target,
    species_share,
):
    params = pltpu.CompilerParams(vmem_limit_bytes=48 * 1024 * 1024)
    shape = jax.ShapeDtypeStruct
    weight, send, cell = pl.pallas_call(
        prepare_kernel,
        name="prepare",
        out_shape=(
            shape((SOURCE, TILE), F32),
            shape((SLOTS * TILES, TILE), BF16),
            shape((1, TILE), F32),
        ),
        in_specs=[VMEM] * 4,
        out_specs=(VMEM,) * 3,
        compiler_params=params,
        cost_estimate=cost(40_000_000, 1_000_000),
    )(dep_frac, dep_slot, dep_off, remap_target)
    interpolate = pl.pallas_call(
        interpolate_kernel,
        name="interpolate",
        out_shape=(shape((2, LEVELS, TILE), F32), shape((PAD, TILE), F32)),
        in_specs=[SMEM, SMEM] + [VMEM] * 8,
        out_specs=(VMEM,) * 2,
        scratch_shapes=[pltpu.VMEM((2, 152, TILE), F32)],
        compiler_params=params,
        cost_estimate=cost(600_000_000, 3_000_000),
    )
    dispatch = pl.pallas_call(
        send_kernel,
        name="dispatch",
        out_shape=(shape((2, LEVELS, TILE), F32), shape((TILES * ROWS, 128), F32)),
        in_specs=[SMEM] + [VMEM] * 8,
        out_specs=(VMEM,) * 2,
        scratch_shapes=[pltpu.VMEM((384, TILE), F32)],
        compiler_params=params,
        cost_estimate=cost(300_000_000, 2_000_000),
    )
    land = pl.pallas_call(
        land_kernel,
        name="land",
        out_shape=shape((2, LEVELS, TILE), F32),
        in_specs=[VMEM] * 2,
        out_specs=VMEM,
        compiler_params=params,
        cost_estimate=cost(300_000_000, 1_500_000),
    )
    current = tracers
    for step_index in range(STEPS):
        pieces = []
        for offset in range(-REACH, REACH + 1):
            if offset == 0:
                pieces.append(current)
            else:
                pieces.append(from_behind(current, "cols", -offset))
        mixed, negative = interpolate(
            dep_blocks, species_share, *pieces, weight, vert_frac, vert_base
        )
        others = [from_behind(negative, "trc", turn) for turn in (1, 3, 2)]
        kept, outgoing = dispatch(
            species_share, mixed, negative, *others, remap_share, send, cell
        )
        arrived = lax.all_to_all(
            outgoing.reshape(TILES, 1, ROWS * 128), "cols", split_axis=0, concat_axis=0, tiled=True
        ).reshape(TILES * ROWS, 128)
        current = land(kept, arrived)
    return current


def solution(mesh):
    return jax.shard_map(
        shards,
        mesh=mesh,
        in_specs=(
            P("trc", None, "cols"),
            P(None, "cols"),
            P(None, "cols"),
            P(None, "cols"),
            P("cols", None, None),
            P("cols"),
            P("cols"),
            P("cols"),
            P("cols"),
            P("trc"),
        ),
        out_specs=P("trc", None, "cols"),
        check_vma=False,
    )
```

```python
import functools

import jax
import jax.numpy as jnp
from jax import lax
from jax.experimental import pallas as pl
from jax.experimental.pallas import tpu as pltpu
from jax.sharding import PartitionSpec as P

BLOCK = 128
REACH = 2
STEPS = 2
LEVELS = 137
TILE = 256
TILES = 128
SLOTS = 4
OFFSETS = 2 * REACH + 1
SOURCE = OFFSETS * BLOCK
ROWS = 9
PAD = 144
HALF = 280
FULL = 552
CELL_LANE = 9
ASK_LANE = 10
VMEM = pl.BlockSpec(memory_space=pltpu.VMEM)
SMEM = pl.BlockSpec(memory_space=pltpu.SMEM)
F32 = jnp.float32
BF16 = jnp.bfloat16


def shift(value, steps):
    pairs = [(source, (source + steps) % TILES) for source in range(TILES)]
    return lax.ppermute(value, "cols", pairs)


def swap_across(value):
    pairs = [(s, (s + 1) % TILES if s % 2 else (s - 1) % TILES) for s in range(TILES)]
    return lax.ppermute(value, "cols", pairs)


def swap_cores(value):
    groups = [[2 * chip, 2 * chip + 1] for chip in range(TILES // 2)]
    return lax.all_to_all(
        value, "cols", split_axis=0, concat_axis=0, tiled=True, axis_index_groups=groups
    )


def cubic_weights(fraction):
    return (
        -fraction * (fraction - 1.0) * (fraction - 2.0) / 6.0,
        (fraction + 1.0) * (fraction - 1.0) * (fraction - 2.0) / 2.0,
        -(fraction + 1.0) * fraction * (fraction - 2.0) / 2.0,
        (fraction + 1.0) * fraction * (fraction - 1.0) / 6.0,
    )


def two_parts(value):
    high = value.astype(BF16)
    return high, (value - high.astype(F32)).astype(BF16)


def pick(index, choices):
    value = jnp.where(index == 1, choices[1], choices[0])
    value = jnp.where(index == 2, choices[2], value)
    return jnp.where(index == 3, choices[3], value)


def prepare_kernel(
    place_ref, frac_ref, slot_ref, off_ref, target_ref, remap_ref, high_ref, low_ref, send_ref, row_ref
):
    core = place_ref[0] & 1
    lon = cubic_weights(frac_ref[0:1, :])
    lat = cubic_weights(frac_ref[1:2, :])
    entry = slot_ref[...].reshape(1, TILE)
    entry = jnp.where((entry & 1) > core, OFFSETS - 1 - entry, entry)
    first = entry * BLOCK + off_ref[...].reshape(1, TILE)
    for part in range(OFFSETS):
        row = lax.broadcasted_iota(jnp.int32, (BLOCK, TILE), 0) + part * BLOCK
        away = row - first
        place = away & 15
        inside = (away >= 0) & (away < 64) & (place < 4)
        weight = jnp.where(inside, pick(away >> 4, lat) * pick(place, lon), 0.0)
        high, low = two_parts(weight)
        high_ref[part * BLOCK : (part + 1) * BLOCK, :] = high
        low_ref[part * BLOCK : (part + 1) * BLOCK, :] = low
    target = target_ref[...].reshape(1, TILE)
    owner = target >> 8
    hit = lax.broadcasted_iota(jnp.int32, (TILES, TILE), 0) == owner
    earlier = lax.broadcasted_iota(jnp.int32, (TILE, TILE), 0) < lax.broadcasted_iota(
        jnp.int32, (TILE, TILE), 1
    )
    one_hot = jnp.where(hit, 1.0, 0.0)
    rank = jnp.dot(
        one_hot.astype(BF16),
        jnp.where(earlier, 1.0, 0.0).astype(BF16),
        preferred_element_type=F32,
    )
    for slot in range(SLOTS):
        chosen = jnp.where(rank == slot, one_hot, 0.0)
        send_ref[slot * TILES : (slot + 1) * TILES, :] = chosen.astype(BF16)
    row_ref[0:1, :] = ((target & (TILE - 1)) + 1).astype(F32)
    row_ref[1:2, :] = remap_ref[...].reshape(1, TILE)
    row_ref[2:8, :] = jnp.zeros((6, TILE), F32)


def interpolate_kernel(
    whole, place_ref, blocks_ref, share_ref, behind, pair, own, across, ahead, high_ref, low_ref,
    frac_ref, base_ref, out_ref, neg_ref, pad_ref,
):
    core = place_ref[0] & 1
    stride = 4 if whole else 2
    rows = FULL if whole else HALF
    at = (0, 3 - 2 * core, 2, 1 + 2 * core, 4)
    skip = (0, (1 - core) * rows, 0, 0, 0)
    high, low = high_ref[...], low_ref[...]
    for n in range(2):
        pieces = []
        for part, source in enumerate((behind, pair, own, across, ahead)):
            if whole or part == 2:
                start = skip[part] + 2 * blocks_ref[at[part]] + n
                pieces.append(source[pl.ds(start, LEVELS, stride=4), :])
            else:
                pieces.append(source[pl.ds(skip[part] + n, LEVELS, stride=stride), :])
        first, second = two_parts(jnp.concatenate(pieces, axis=1))
        pad_ref[n, 0:8, :] = jnp.zeros((8, TILE), F32)
        pad_ref[n, 144:152, :] = jnp.zeros((8, TILE), F32)
        pad_ref[n, 8 : 8 + LEVELS, :] = (
            jnp.dot(second, high, preferred_element_type=F32)
            + jnp.dot(first, low, preferred_element_type=F32)
        ) + jnp.dot(first, high, preferred_element_type=F32)
    vert = cubic_weights(frac_ref[...])
    level = lax.broadcasted_iota(jnp.int32, (LEVELS, TILE), 0)
    away = base_ref[...] - level
    same = [away == delta for delta in range(-3, 2)]
    total = [jnp.zeros((LEVELS, TILE), F32), jnp.zeros((LEVELS, TILE), F32)]
    for delta in range(-3, 5):
        factor = jnp.zeros((LEVELS, TILE), F32)
        for tap in range(4):
            if -3 <= delta - tap <= 1:
                factor = jnp.where(same[delta - tap + 3], vert[tap], factor)
        for n in range(2):
            total[n] = total[n] + factor * pad_ref[n, 8 + delta : 8 + delta + LEVELS, :]
    out_ref[0] = total[0]
    out_ref[1] = total[1]
    negative = jnp.minimum(total[0], 0.0) + jnp.minimum(total[1], 0.0)
    share = jnp.full((8, TILE), share_ref[0] + share_ref[1], F32)
    for copy in range(4):
        neg_ref[copy, 136:PAD, :] = share
        neg_ref[copy, 0:LEVELS, :] = negative


def send_kernel(
    place_ref, blocks_ref, share_ref, mixed_ref, parts_ref, send_ref, row_ref, kept_ref, out_ref, x_ref
):
    all_parts = (parts_ref[0] + parts_ref[1]) + (parts_ref[2] + parts_ref[3])
    deficit = all_parts[0:LEVELS, :]
    whole = all_parts[LEVELS : LEVELS + 1, :]
    remap = row_ref[1:2, :]
    x_ref[256:384, :] = jnp.zeros((128, TILE), F32)
    for n in range(2):
        fixed = jnp.maximum(mixed_ref[n], 0.0) + (share_ref[n] / whole) * deficit
        kept_ref[n] = (1.0 - remap) * fixed
        moved = remap * fixed
        x_ref[n * 128 : n * 128 + 128, :] = moved[0:128, :]
        x_ref[256 + 16 * n : 256 + 16 * n + 9, :] = moved[128:LEVELS, :]
    x_ref[256 + CELL_LANE : 257 + CELL_LANE, :] = row_ref[0:1, :]
    send = send_ref[...]
    dims = (((1,), (1,)), ((), ()))
    first, second = two_parts(x_ref[...])
    result = lax.dot_general(send, second, dims, preferred_element_type=F32)
    result = result + lax.dot_general(send, first, dims, preferred_element_type=F32)
    tile = lax.broadcasted_iota(jnp.int32, (TILES, 128), 0)
    asked = jnp.zeros((TILES, 128), F32)
    for part in range(OFFSETS):
        if part != REACH:
            reader = (place_ref[0] + part - REACH) & (TILES - 1)
            asked = jnp.where(tile == reader, blocks_ref[part].astype(F32), asked)
    lane = lax.broadcasted_iota(jnp.int32, (TILES, 128), 1)
    rest = jnp.where(lane == ASK_LANE, asked, 0.0)
    for slot in range(SLOTS):
        rows = result[slot * TILES : (slot + 1) * TILES, :]
        for n in range(2):
            out_ref[pl.ds(2 * slot + n, TILES, stride=ROWS), :] = rows[:, n * 128 : n * 128 + 128]
        tail = rows[:, 256:384]
        if slot:
            tail = pltpu.roll(tail, 32 * slot, axis=1)
        rest = rest + tail
    out_ref[pl.ds(8, TILES, stride=ROWS), :] = rest


def landed(got_ref):
    rest = got_ref[pl.ds(8, TILES, stride=ROWS), :].T
    column = (lax.broadcasted_iota(jnp.int32, (TILE, TILES), 0) + 1).astype(F32)
    sums = [None, None]
    tails = [None, None]
    for slot in range(SLOTS):
        cell = rest[32 * slot + CELL_LANE : 32 * slot + CELL_LANE + 1, :]
        landing = jnp.where(column == cell, 1.0, 0.0).astype(BF16)
        for n in range(2):
            for piece in two_parts(got_ref[pl.ds(2 * slot + n, TILES, stride=ROWS), :]):
                term = jnp.dot(landing, piece, preferred_element_type=F32)
                sums[n] = term if sums[n] is None else sums[n] + term
            tail = rest[32 * slot + 16 * n : 32 * slot + 16 * n + 16, :]
            for piece in two_parts(tail):
                term = lax.dot_general(
                    piece, landing, (((1,), (1,)), ((), ())), preferred_element_type=F32
                )
                tails[n] = term if tails[n] is None else tails[n] + term
    return [value.T for value in sums], [value[0 : LEVELS - 128, :] for value in tails]


def land_kernel(kept_ref, got_ref, out_ref):
    sums, tails = landed(got_ref)
    for n in range(2):
        upper = kept_ref[n, 0:128, :] + sums[n]
        lower = kept_ref[n, 128:LEVELS, :] + tails[n]
        for block in range(2):
            lanes = slice(block * BLOCK, (block + 1) * BLOCK)
            out_ref[pl.ds(2 * block + n, 128, stride=4), :] = upper[:, lanes]
            out_ref[pl.ds(512 + 2 * block + n, LEVELS - 128, stride=4), :] = lower[:, lanes]


def land_and_select_kernel(
    place_ref, kept_ref, got_ref, out_ref, behind_ref, pair_ref, across_ref, ahead_ref
):
    place = place_ref[0]
    core = place & 1
    readers = (place + 2, place + 1 - 2 * core, place - 1 + 2 * core, place - 2)
    asks = []
    for reader in readers:
        row = (reader & (TILES - 1)) * ROWS + 8
        asks.append(got_ref[pl.ds(row, 1), :][:, ASK_LANE : ASK_LANE + 1] > 0.5)
    sums, tails = landed(got_ref)
    for n in range(2):
        for begin, count, values in ((0, 128, sums[n]), (128, LEVELS - 128, tails[n])):
            value = kept_ref[n, begin : begin + count, :] + values
            left, right = value[:, 0:BLOCK], value[:, BLOCK:TILE]
            out_ref[pl.ds(4 * begin + n, count, stride=4), :] = left
            out_ref[pl.ds(4 * begin + 2 + n, count, stride=4), :] = right
            for ask, ref in zip(asks, (behind_ref, pair_ref, across_ref, ahead_ref)):
                chosen = jnp.where(ask, right, left)
                ref[pl.ds(2 * begin + n, count, stride=2), :] = chosen
                if ref is pair_ref:
                    ref[pl.ds(HALF + 2 * begin + n, count, stride=2), :] = chosen


def cost(flops, moved):
    return pl.CostEstimate(flops=flops, bytes_accessed=moved, transcendentals=0)


def shards(
    tracers,
    dep_frac,
    vert_frac,
    vert_base,
    dep_blocks,
    dep_slot,
    dep_off,
    remap_share,
    remap_target,
    species_share,
):
    params = pltpu.CompilerParams(vmem_limit_bytes=48 * 1024 * 1024)
    shape = jax.ShapeDtypeStruct
    place = lax.axis_index("cols").astype(jnp.int32).reshape(1)
    dep_blocks = dep_blocks.reshape(OFFSETS)
    own = jnp.pad(tracers, ((0, 0), (0, FULL // 4 - LEVELS), (0, 0)))
    own = own.reshape(2, FULL // 4, 2, BLOCK).transpose(1, 2, 0, 3).reshape(FULL, BLOCK)
    own, place, dep_blocks = lax.optimization_barrier((own, place, dep_blocks))
    high, low, send, row = pl.pallas_call(
        prepare_kernel,
        name="prepare",
        out_shape=(
            shape((SOURCE, TILE), BF16),
            shape((SOURCE, TILE), BF16),
            shape((SLOTS * TILES, TILE), BF16),
            shape((8, TILE), F32),
        ),
        in_specs=[SMEM] + [VMEM] * 5,
        out_specs=(VMEM,) * 4,
        compiler_params=params,
        cost_estimate=cost(40_000_000, 1_000_000),
    )(place, dep_frac, dep_slot, dep_off, remap_target, remap_share)

    def interpolate(whole, *sources):
        return pl.pallas_call(
            functools.partial(interpolate_kernel, whole),
            name="interpolate",
            out_shape=(shape((2, LEVELS, TILE), F32), shape((4, PAD, TILE), F32)),
            in_specs=[SMEM] * 3 + [VMEM] * 9,
            out_specs=(VMEM,) * 2,
            scratch_shapes=[pltpu.VMEM((2, 152, TILE), F32)],
            compiler_params=params,
            cost_estimate=cost(400_000_000, 3_000_000),
        )(place, dep_blocks, species_share, *sources, high, low, vert_frac, vert_base)

    dispatch = pl.pallas_call(
        send_kernel,
        name="dispatch",
        out_shape=(shape((2, LEVELS, TILE), F32), shape((TILES * ROWS, 128), F32)),
        in_specs=[SMEM] * 3 + [VMEM] * 4,
        out_specs=(VMEM,) * 2,
        scratch_shapes=[pltpu.VMEM((384, TILE), F32)],
        compiler_params=params,
        cost_estimate=cost(200_000_000, 2_000_000),
    )
    land = pl.pallas_call(
        land_kernel,
        name="land",
        out_shape=shape((FULL, 128), F32),
        in_specs=[VMEM] * 2,
        out_specs=VMEM,
        compiler_params=params,
        cost_estimate=cost(200_000_000, 1_500_000),
    )
    land_and_select = pl.pallas_call(
        land_and_select_kernel,
        name="land_and_select",
        out_shape=(
            shape((FULL, 128), F32),
            shape((HALF, 128), F32),
            shape((2 * HALF, 128), F32),
            shape((HALF, 128), F32),
            shape((HALF, 128), F32),
        ),
        in_specs=[SMEM] + [VMEM] * 2,
        out_specs=(VMEM,) * 5,
        compiler_params=params,
        cost_estimate=cost(200_000_000, 2_500_000),
    )
    to_behind, to_pair, to_across, to_ahead = own, jnp.concatenate([own, own]), own, own
    for step_index in range(STEPS):
        across = swap_across(to_across)
        behind = shift(to_behind, 2)
        ahead = shift(to_ahead, -2)
        half = to_pair.shape[0] // 2
        pair = swap_cores(to_pair.reshape(2, half, BLOCK)).reshape(2 * half, BLOCK)
        mixed, negative = interpolate(step_index == 0, behind, pair, own, across, ahead)
        parts = lax.all_to_all(negative, "trc", split_axis=0, concat_axis=0, tiled=True)
        kept, outgoing = dispatch(
            place, dep_blocks, species_share, mixed, parts, send, row
        )
        arrived = lax.all_to_all(
            outgoing.reshape(TILES, 1, ROWS * 128), "cols", split_axis=0, concat_axis=0, tiled=True
        ).reshape(TILES * ROWS, 128)
        if step_index + 1 < STEPS:
            own, to_behind, to_pair, to_across, to_ahead = land_and_select(place, kept, arrived)
        else:
            own = land(kept, arrived)
    out = own.reshape(FULL // 4, 2, 2, BLOCK)[:LEVELS]
    return out.transpose(2, 0, 1, 3).reshape(2, LEVELS, TILE)


def solution(mesh):
    return jax.shard_map(
        shards,
        mesh=mesh,
        in_specs=(
            P("trc", None, "cols"),
            P(None, "cols"),
            P(None, "cols"),
            P(None, "cols"),
            P("cols", None, None),
            P("cols"),
            P("cols"),
            P("cols"),
            P("cols"),
            P("trc"),
        ),
        out_specs=P("trc", None, "cols"),
        check_vma=False,
    )
```

```python
import functools

import jax
import jax.numpy as jnp
from jax import lax
from jax.experimental import pallas as pl
from jax.experimental.pallas import tpu as pltpu
from jax.sharding import PartitionSpec as P

BLOCK = 128
REACH = 2
STEPS = 2
LEVELS = 137
TILE = 256
TILES = 128
SLOTS = 4
OFFSETS = 2 * REACH + 1
SOURCE = OFFSETS * BLOCK
ROWS = 9
PAD = 144
HALF = 280
FULL = 4 * LEVELS
CELL_LANE = 9
ASK_LANE = 10
VMEM = pl.BlockSpec(memory_space=pltpu.VMEM)
F32 = jnp.float32
BF16 = jnp.bfloat16


def shift(value, steps):
    pairs = [(source, (source + steps) % TILES) for source in range(TILES)]
    return lax.ppermute(value, "cols", pairs)


def swap_across(value):
    pairs = [(s, (s + 1) % TILES if s % 2 else (s - 1) % TILES) for s in range(TILES)]
    return lax.ppermute(value, "cols", pairs)


def swap_cores(value):
    groups = [[2 * chip, 2 * chip + 1] for chip in range(TILES // 2)]
    return lax.all_to_all(
        value, "cols", split_axis=0, concat_axis=0, tiled=True, axis_index_groups=groups
    )


def cubic_weights(fraction):
    return (
        -fraction * (fraction - 1.0) * (fraction - 2.0) / 6.0,
        (fraction + 1.0) * (fraction - 1.0) * (fraction - 2.0) / 2.0,
        -(fraction + 1.0) * fraction * (fraction - 2.0) / 2.0,
        (fraction + 1.0) * fraction * (fraction - 1.0) / 6.0,
    )


def two_parts(value):
    high = value.astype(BF16)
    return high, (value - high.astype(F32)).astype(BF16)


def pick(index, choices):
    value = jnp.where(index == 1, choices[1], choices[0])
    value = jnp.where(index == 2, choices[2], value)
    return jnp.where(index == 3, choices[3], value)


def prepare_kernel(
    frac_in, slot_in, off_in, target_in, remap_in, blocks_in, share_in, vert_in, base_in, own_in,
    high_ref, low_ref, factor_ref, send_ref, row_ref, mask_ref, asked_ref, own_ref,
    frac_ref, slot_ref, off_ref, target_ref, remap_ref, blocks_ref, share_ref, vert_ref, base_ref, sems,
):
    arrays = (
        frac_in, slot_in, off_in, target_in, remap_in, blocks_in, share_in, vert_in, base_in,
        own_in, own_in,
    )
    places = (
        frac_ref, slot_ref, off_ref, target_ref, remap_ref, blocks_ref, share_ref, vert_ref, base_ref,
        own_ref.at[0], own_ref.at[1],
    )
    copies = [
        pltpu.make_async_copy(array, there, sems.at[at])
        for at, (array, there) in enumerate(zip(arrays, places))
    ]
    for copy in copies:
        copy.start()
    for copy in copies[:9]:
        copy.wait()
    place = lax.axis_index("cols")
    core = place & 1
    lon = cubic_weights(frac_ref[0:1, :])
    lat = cubic_weights(frac_ref[1:2, :])
    entry = slot_ref[...].reshape(1, TILE)
    entry = jnp.where((entry & 1) > core, OFFSETS - 1 - entry, entry)
    first = entry * BLOCK + off_ref[...].reshape(1, TILE)
    for part in range(OFFSETS):
        row = lax.broadcasted_iota(jnp.int32, (BLOCK, TILE), 0) + part * BLOCK
        away = row - first
        column = away & 15
        inside = (away >= 0) & (away < 64) & (column < 4)
        weight = jnp.where(inside, pick(away >> 4, lat) * pick(column, lon), 0.0)
        high, low = two_parts(weight)
        high_ref[part * BLOCK : (part + 1) * BLOCK, :] = high
        low_ref[part * BLOCK : (part + 1) * BLOCK, :] = low
    vert = cubic_weights(vert_ref[...])
    away = base_ref[...] - lax.broadcasted_iota(jnp.int32, (LEVELS, TILE), 0)
    same = [away == delta for delta in range(-3, 2)]
    for delta in range(-3, 5):
        factor = jnp.zeros((LEVELS, TILE), F32)
        for tap in range(4):
            if -3 <= delta - tap <= 1:
                factor = jnp.where(same[delta - tap + 3], vert[tap], factor)
        factor_ref[delta + 3] = factor
    target = target_ref[...].reshape(1, TILE)
    owner = target >> 8
    hit = lax.broadcasted_iota(jnp.int32, (TILES, TILE), 0) == owner
    earlier = lax.broadcasted_iota(jnp.int32, (TILE, TILE), 0) < lax.broadcasted_iota(
        jnp.int32, (TILE, TILE), 1
    )
    one_hot = jnp.where(hit, 1.0, 0.0)
    rank = jnp.dot(
        one_hot.astype(BF16),
        jnp.where(earlier, 1.0, 0.0).astype(BF16),
        preferred_element_type=F32,
    )
    for slot in range(SLOTS):
        chosen = jnp.where(rank == slot, one_hot, 0.0)
        send_ref[slot * TILES : (slot + 1) * TILES, :] = chosen.astype(BF16)
    row_ref[0:1, :] = ((target & (TILE - 1)) + 1).astype(F32)
    row_ref[1:2, :] = remap_ref[...].reshape(1, TILE)
    row_ref[2:3, :] = jnp.full((1, TILE), share_ref[0], F32)
    row_ref[3:4, :] = jnp.full((1, TILE), share_ref[1], F32)
    row_ref[4:8, :] = jnp.zeros((4, TILE), F32)
    marks = [blocks_ref[at] for at in (0, 3 - 2 * core, 2, 1 + 2 * core, 4)] + [core]
    for at, mark in enumerate(marks):
        mask_ref[at : at + 1, :] = jnp.full((1, 128), mark, jnp.int32).astype(F32)
    mask_ref[6:8, :] = jnp.zeros((2, 128), F32)
    tile = lax.broadcasted_iota(jnp.int32, (1, 128), 1)
    for at, reader in enumerate((place + 2, place + 1 - 2 * core, place - 1 + 2 * core, place - 2)):
        mask_ref[8 + at : 9 + at, :] = jnp.where(tile == (reader & (TILES - 1)), 1.0, 0.0)
    mask_ref[12:16, :] = jnp.zeros((4, 128), F32)
    tile = lax.broadcasted_iota(jnp.int32, (TILES, 128), 0)
    asked = jnp.zeros((TILES, 128), F32)
    for part in range(OFFSETS):
        if part != REACH:
            reader = (place + part - REACH) & (TILES - 1)
            asked = jnp.where(tile == reader, blocks_ref[part].astype(F32), asked)
    lane = lax.broadcasted_iota(jnp.int32, (TILES, 128), 1)
    asked_ref[...] = jnp.where(lane == ASK_LANE, asked, 0.0)
    for copy in copies[9:]:
        copy.wait()


def interpolate_kernel(
    whole, behind, pair, own, across, ahead, high_ref, low_ref, factor_ref, row_ref, mask_ref,
    out_ref, neg_ref, pad_ref,
):
    high, low = high_ref[...], low_ref[...]
    second_core = mask_ref[5:6, :] > 0.5
    for n in range(2):
        pieces = []
        for part, source in enumerate((behind, pair, own, across, ahead)):
            if whole and part == 1:
                flat = source.reshape(2 * FULL, BLOCK)
                blocks = [
                    jnp.where(
                        second_core,
                        flat[pl.ds(2 * block + n, LEVELS, stride=4), :],
                        flat[pl.ds(FULL + 2 * block + n, LEVELS, stride=4), :],
                    )
                    for block in range(2)
                ]
                piece = jnp.where(mask_ref[part : part + 1, :] > 0.5, blocks[1], blocks[0])
            elif whole or part == 2:
                flat = (source.at[0] if whole and part == 2 else source).reshape(FULL, BLOCK)
                piece = jnp.where(
                    mask_ref[part : part + 1, :] > 0.5,
                    flat[pl.ds(2 + n, LEVELS, stride=4), :],
                    flat[pl.ds(n, LEVELS, stride=4), :],
                )
            elif part == 1:
                piece = jnp.where(
                    second_core,
                    source[pl.ds(n, LEVELS, stride=2), :],
                    source[pl.ds(HALF + n, LEVELS, stride=2), :],
                )
            else:
                piece = source[pl.ds(n, LEVELS, stride=2), :]
            pieces.append(piece)
        first, second = two_parts(jnp.concatenate(pieces, axis=1))
        pad_ref[n, 0:8, :] = jnp.zeros((8, TILE), F32)
        pad_ref[n, 144:152, :] = jnp.zeros((8, TILE), F32)
        pad_ref[n, 8 : 8 + LEVELS, :] = (
            jnp.dot(second, high, preferred_element_type=F32)
            + jnp.dot(first, low, preferred_element_type=F32)
        ) + jnp.dot(first, high, preferred_element_type=F32)
    total = [jnp.zeros((LEVELS, TILE), F32), jnp.zeros((LEVELS, TILE), F32)]
    for delta in range(-3, 5):
        factor = factor_ref[delta + 3]
        for n in range(2):
            total[n] = total[n] + factor * pad_ref[n, 8 + delta : 8 + delta + LEVELS, :]
    out_ref[0] = total[0]
    out_ref[1] = total[1]
    negative = jnp.minimum(total[0], 0.0) + jnp.minimum(total[1], 0.0)
    share = jnp.broadcast_to(row_ref[2:3, :] + row_ref[3:4, :], (8, TILE))
    for copy in range(4):
        neg_ref[copy, 136:PAD, :] = share
        neg_ref[copy, 0:LEVELS, :] = negative


def send_kernel(mixed_ref, parts_ref, send_ref, row_ref, asked_ref, kept_ref, out_ref, x_ref):
    all_parts = (parts_ref[0] + parts_ref[1]) + (parts_ref[2] + parts_ref[3])
    deficit = all_parts[0:LEVELS, :]
    whole = all_parts[LEVELS : LEVELS + 1, :]
    remap = row_ref[1:2, :]
    x_ref[256:384, :] = jnp.zeros((128, TILE), F32)
    for n in range(2):
        fixed = jnp.maximum(mixed_ref[n], 0.0) + (row_ref[2 + n : 3 + n, :] / whole) * deficit
        kept_ref[n] = (1.0 - remap) * fixed
        moved = remap * fixed
        x_ref[n * 128 : n * 128 + 128, :] = moved[0:128, :]
        x_ref[256 + 16 * n : 256 + 16 * n + 9, :] = moved[128:LEVELS, :]
    x_ref[256 + CELL_LANE : 257 + CELL_LANE, :] = row_ref[0:1, :]
    send = send_ref[...]
    dims = (((1,), (1,)), ((), ()))
    first, second = two_parts(x_ref[...])
    result = lax.dot_general(send, second, dims, preferred_element_type=F32)
    result = result + lax.dot_general(send, first, dims, preferred_element_type=F32)
    rest = asked_ref[...]
    for slot in range(SLOTS):
        rows = result[slot * TILES : (slot + 1) * TILES, :]
        for n in range(2):
            out_ref[pl.ds(2 * slot + n, TILES, stride=ROWS), :] = rows[:, n * 128 : n * 128 + 128]
        tail = rows[:, 256:384]
        if slot:
            tail = pltpu.roll(tail, 32 * slot, axis=1)
        rest = rest + tail
    out_ref[pl.ds(8, TILES, stride=ROWS), :] = rest


def landed(got_ref):
    rest = got_ref[pl.ds(8, TILES, stride=ROWS), :].T
    column = (lax.broadcasted_iota(jnp.int32, (TILE, TILES), 0) + 1).astype(F32)
    sums = [None, None]
    tails = [None, None]
    for slot in range(SLOTS):
        cell = rest[32 * slot + CELL_LANE : 32 * slot + CELL_LANE + 1, :]
        landing = jnp.where(column == cell, 1.0, 0.0).astype(BF16)
        for n in range(2):
            for piece in two_parts(got_ref[pl.ds(2 * slot + n, TILES, stride=ROWS), :]):
                term = jnp.dot(landing, piece, preferred_element_type=F32)
                sums[n] = term if sums[n] is None else sums[n] + term
            tail = rest[32 * slot + 16 * n : 32 * slot + 16 * n + 16, :]
            for piece in two_parts(tail):
                term = lax.dot_general(
                    piece, landing, (((1,), (1,)), ((), ())), preferred_element_type=F32
                )
                tails[n] = term if tails[n] is None else tails[n] + term
    tails = [value[0 : LEVELS - 128, :] for value in tails]
    return [value.T for value in sums], tails, rest[ASK_LANE : ASK_LANE + 1, :]


def land_kernel(kept_ref, got_ref, out_ref):
    sums, tails, _ = landed(got_ref)
    flat = out_ref.reshape(FULL, BLOCK)
    for n in range(2):
        upper = kept_ref[n, 0:128, :] + sums[n]
        lower = kept_ref[n, 128:LEVELS, :] + tails[n]
        for block in range(2):
            lanes = slice(block * BLOCK, (block + 1) * BLOCK)
            flat[pl.ds(2 * block + n, 128, stride=4), :] = upper[:, lanes]
            flat[pl.ds(512 + 2 * block + n, LEVELS - 128, stride=4), :] = lower[:, lanes]


def land_and_select_kernel(
    kept_ref, got_ref, mask_ref, out_ref, behind_ref, pair_ref, across_ref, ahead_ref
):
    sums, tails, asked = landed(got_ref)
    flat = out_ref.reshape(FULL, BLOCK)
    wanted = jnp.sum(mask_ref[8:16, :] * asked, axis=1, keepdims=True)
    asks = [wanted[at : at + 1, :] > 0.5 for at in range(4)]
    for n in range(2):
        for begin, count, values in ((0, 128, sums[n]), (128, LEVELS - 128, tails[n])):
            value = kept_ref[n, begin : begin + count, :] + values
            left, right = value[:, 0:BLOCK], value[:, BLOCK:TILE]
            flat[pl.ds(4 * begin + n, count, stride=4), :] = left
            flat[pl.ds(4 * begin + 2 + n, count, stride=4), :] = right
            for ask, ref in zip(asks, (behind_ref, pair_ref, across_ref, ahead_ref)):
                chosen = jnp.where(ask, right, left)
                ref[pl.ds(2 * begin + n, count, stride=2), :] = chosen
                if ref is pair_ref:
                    ref[pl.ds(HALF + 2 * begin + n, count, stride=2), :] = chosen


def cost(flops, moved):
    return pl.CostEstimate(flops=flops, bytes_accessed=moved, transcendentals=0)


def shards(
    tracers,
    dep_frac,
    vert_frac,
    vert_base,
    dep_blocks,
    dep_slot,
    dep_off,
    remap_share,
    remap_target,
    species_share,
):
    params = pltpu.CompilerParams(vmem_limit_bytes=48 * 1024 * 1024)
    shape = jax.ShapeDtypeStruct
    own = tracers.reshape(2, LEVELS, 2, BLOCK).transpose(1, 2, 0, 3).reshape(LEVELS, 4, BLOCK)
    to_behind, to_across, to_ahead = own, own, own
    high, low, factor, send, row, mask, asked, doubled = pl.pallas_call(
        prepare_kernel,
        name="prepare",
        out_shape=(
            shape((SOURCE, TILE), BF16),
            shape((SOURCE, TILE), BF16),
            shape((8, LEVELS, TILE), F32),
            shape((SLOTS * TILES, TILE), BF16),
            shape((8, TILE), F32),
            shape((16, 128), F32),
            shape((TILES, 128), F32),
            shape((2, LEVELS, 4, BLOCK), F32),
        ),
        in_specs=[pl.BlockSpec(memory_space=pltpu.MemorySpace.HBM)] * 10,
        out_specs=(VMEM,) * 8,
        scratch_shapes=[
            pltpu.VMEM((2, TILE), F32),
            pltpu.VMEM((TILE,), jnp.int32),
            pltpu.VMEM((TILE,), jnp.int32),
            pltpu.VMEM((TILE,), jnp.int32),
            pltpu.VMEM((TILE,), F32),
            pltpu.SMEM((OFFSETS,), jnp.int32),
            pltpu.SMEM((2,), F32),
            pltpu.VMEM((LEVELS, TILE), F32),
            pltpu.VMEM((LEVELS, TILE), jnp.int32),
            pltpu.SemaphoreType.DMA((11,)),
        ],
        compiler_params=params,
        cost_estimate=cost(40_000_000, 2_000_000),
    )(
        *[
            pltpu.with_memory_space_constraint(value, pltpu.MemorySpace.HBM)
            for value in (
                dep_frac, dep_slot, dep_off, remap_target, remap_share, dep_blocks.reshape(OFFSETS),
                species_share, vert_frac, vert_base, own,
            )
        ]
    )

    def interpolate(whole, *sources):
        return pl.pallas_call(
            functools.partial(interpolate_kernel, whole),
            name="interpolate",
            out_shape=(shape((2, LEVELS, TILE), F32), shape((4, PAD, TILE), F32)),
            in_specs=[VMEM] * 10,
            out_specs=(VMEM,) * 2,
            scratch_shapes=[pltpu.VMEM((2, 152, TILE), F32)],
            compiler_params=params,
            cost_estimate=cost(400_000_000, 3_000_000),
        )(*sources, high, low, factor, row, mask)

    dispatch = pl.pallas_call(
        send_kernel,
        name="dispatch",
        out_shape=(shape((2, LEVELS, TILE), F32), shape((TILES * ROWS, 128), F32)),
        in_specs=[VMEM] * 5,
        out_specs=(VMEM,) * 2,
        scratch_shapes=[pltpu.VMEM((384, TILE), F32)],
        compiler_params=params,
        cost_estimate=cost(200_000_000, 2_000_000),
    )
    land = pl.pallas_call(
        land_kernel,
        name="land",
        out_shape=shape((LEVELS, 4, BLOCK), F32),
        in_specs=[VMEM] * 2,
        out_specs=VMEM,
        compiler_params=params,
        cost_estimate=cost(200_000_000, 1_500_000),
    )
    land_and_select = pl.pallas_call(
        land_and_select_kernel,
        name="land_and_select",
        out_shape=(
            shape((LEVELS, 4, BLOCK), F32),
            shape((HALF, 128), F32),
            shape((2 * HALF, 128), F32),
            shape((HALF, 128), F32),
            shape((HALF, 128), F32),
        ),
        in_specs=[VMEM] * 3,
        out_specs=(VMEM,) * 5,
        compiler_params=params,
        cost_estimate=cost(200_000_000, 2_500_000),
    )
    for step_index in range(STEPS):
        across = swap_across(to_across)
        behind = shift(to_behind, 2)
        ahead = shift(to_ahead, -2)
        if step_index == 0:
            pair, own = swap_cores(doubled), doubled
        else:
            pair = swap_cores(to_pair.reshape(2, HALF, BLOCK)).reshape(2 * HALF, BLOCK)
        mixed, negative = interpolate(step_index == 0, behind, pair, own, across, ahead)
        parts = lax.all_to_all(negative, "trc", split_axis=0, concat_axis=0, tiled=True)
        kept, outgoing = dispatch(mixed, parts, send, row, asked)
        arrived = lax.all_to_all(
            outgoing.reshape(TILES, 1, ROWS * 128), "cols", split_axis=0, concat_axis=0, tiled=True
        ).reshape(TILES * ROWS, 128)
        if step_index + 1 < STEPS:
            own, to_behind, to_pair, to_across, to_ahead = land_and_select(kept, arrived, mask)
        else:
            own = land(kept, arrived)
    out = own.reshape(LEVELS, 2, 2, BLOCK).transpose(2, 0, 1, 3)
    return out.reshape(2, LEVELS, TILE)


def solution(mesh):
    return jax.shard_map(
        shards,
        mesh=mesh,
        in_specs=(
            P("trc", None, "cols"),
            P(None, "cols"),
            P(None, "cols"),
            P(None, "cols"),
            P("cols", None, None),
            P("cols"),
            P("cols"),
            P("cols"),
            P("cols"),
            P("trc"),
        ),
        out_specs=P("trc", None, "cols"),
        check_vma=False,
    )
```

```python
import functools

import jax
import jax.numpy as jnp
from jax import lax
from jax.experimental import pallas as pl
from jax.experimental.pallas import tpu as pltpu
from jax.sharding import PartitionSpec as P

BLOCK = 128
REACH = 2
STEPS = 2
LEVELS = 137
TILE = 256
TILES = 128
SLOTS = 4
OFFSETS = 2 * REACH + 1
SOURCE = OFFSETS * BLOCK
ROWS = 9
PAD = 144
HALF = 280
FULL = 4 * LEVELS
CELL_LANE = 9
ASK_LANE = 10
VMEM = pl.BlockSpec(memory_space=pltpu.VMEM)
F32 = jnp.float32
BF16 = jnp.bfloat16


def swap_chips(value, low):
    pairs = []
    for chip in range(low, TILES // 2 + low, 2):
        for core in range(2):
            here, there = (2 * chip + core) % TILES, (2 * chip + 2 + core) % TILES
            pairs += [(here, there), (there, here)]
    return lax.ppermute(value, "cols", sorted(pairs))


def swap_across(value):
    pairs = [(s, (s + 1) % TILES if s % 2 else (s - 1) % TILES) for s in range(TILES)]
    return lax.ppermute(value, "cols", pairs)


def swap_cores(value):
    groups = [[2 * chip, 2 * chip + 1] for chip in range(TILES // 2)]
    return lax.all_to_all(
        value, "cols", split_axis=0, concat_axis=0, tiled=True, axis_index_groups=groups
    )


def cubic_weights(fraction):
    return (
        -fraction * (fraction - 1.0) * (fraction - 2.0) / 6.0,
        (fraction + 1.0) * (fraction - 1.0) * (fraction - 2.0) / 2.0,
        -(fraction + 1.0) * fraction * (fraction - 2.0) / 2.0,
        (fraction + 1.0) * fraction * (fraction - 1.0) / 6.0,
    )


def two_parts(value):
    high = value.astype(BF16)
    return high, (value - high.astype(F32)).astype(BF16)


def pick(index, choices):
    value = jnp.where(index == 1, choices[1], choices[0])
    value = jnp.where(index == 2, choices[2], value)
    return jnp.where(index == 3, choices[3], value)


def prepare_kernel(
    frac_in, slot_in, off_in, target_in, remap_in, blocks_in, share_in, vert_in, base_in, own_in,
    high_ref, low_ref, factor_ref, send_ref, row_ref, mask_ref, asked_ref, own_ref,
    frac_ref, slot_ref, off_ref, target_ref, remap_ref, blocks_ref, share_ref, vert_ref, base_ref, sems,
):
    arrays = (
        frac_in, slot_in, off_in, target_in, remap_in, blocks_in, share_in, vert_in, base_in,
        own_in, own_in,
    )
    places = (
        frac_ref, slot_ref, off_ref, target_ref, remap_ref, blocks_ref, share_ref, vert_ref, base_ref,
        own_ref.at[0], own_ref.at[1],
    )
    copies = [
        pltpu.make_async_copy(array, there, sems.at[at])
        for at, (array, there) in enumerate(zip(arrays, places))
    ]
    for copy in copies:
        copy.start()
    for copy in copies[:9]:
        copy.wait()
    place = lax.axis_index("cols")
    core = place & 1
    odd = (place >> 1) & 1
    lon = cubic_weights(frac_ref[0:1, :])
    lat = cubic_weights(frac_ref[1:2, :])
    entry = slot_ref[...].reshape(1, TILE)
    turned = jnp.where((entry & 1) == 1, 1 - core, odd)
    entry = jnp.where(turned == 1, OFFSETS - 1 - entry, entry)
    first = entry * BLOCK + off_ref[...].reshape(1, TILE)
    for part in range(OFFSETS):
        row = lax.broadcasted_iota(jnp.int32, (BLOCK, TILE), 0) + part * BLOCK
        away = row - first
        column = away & 15
        inside = (away >= 0) & (away < 64) & (column < 4)
        weight = jnp.where(inside, pick(away >> 4, lat) * pick(column, lon), 0.0)
        high, low = two_parts(weight)
        high_ref[part * BLOCK : (part + 1) * BLOCK, :] = high
        low_ref[part * BLOCK : (part + 1) * BLOCK, :] = low
    vert = cubic_weights(vert_ref[...])
    away = base_ref[...] - lax.broadcasted_iota(jnp.int32, (LEVELS, TILE), 0)
    same = [away == delta for delta in range(-3, 2)]
    for delta in range(-3, 5):
        factor = jnp.zeros((LEVELS, TILE), F32)
        for tap in range(4):
            if -3 <= delta - tap <= 1:
                factor = jnp.where(same[delta - tap + 3], vert[tap], factor)
        factor_ref[delta + 3] = factor
    target = target_ref[...].reshape(1, TILE)
    owner = target >> 8
    hit = lax.broadcasted_iota(jnp.int32, (TILES, TILE), 0) == owner
    earlier = lax.broadcasted_iota(jnp.int32, (TILE, TILE), 0) < lax.broadcasted_iota(
        jnp.int32, (TILE, TILE), 1
    )
    one_hot = jnp.where(hit, 1.0, 0.0)
    rank = jnp.dot(
        one_hot.astype(BF16),
        jnp.where(earlier, 1.0, 0.0).astype(BF16),
        preferred_element_type=F32,
    )
    for slot in range(SLOTS):
        chosen = jnp.where(rank == slot, one_hot, 0.0)
        send_ref[slot * TILES : (slot + 1) * TILES, :] = chosen.astype(BF16)
    row_ref[0:1, :] = ((target & (TILE - 1)) + 1).astype(F32)
    row_ref[1:2, :] = remap_ref[...].reshape(1, TILE)
    row_ref[2:3, :] = jnp.full((1, TILE), share_ref[0], F32)
    row_ref[3:4, :] = jnp.full((1, TILE), share_ref[1], F32)
    row_ref[4:8, :] = jnp.zeros((4, TILE), F32)
    marks = [blocks_ref[at] for at in (4 * odd, 3 - 2 * core, 2, 1 + 2 * core, 4 - 4 * odd)] + [core]
    for at, mark in enumerate(marks):
        mask_ref[at : at + 1, :] = jnp.full((1, 128), mark, jnp.int32).astype(F32)
    mask_ref[6:8, :] = jnp.zeros((2, 128), F32)
    tile = lax.broadcasted_iota(jnp.int32, (1, 128), 1)
    for at, reader in enumerate(
        (place - 2 + 4 * odd, place + 1 - 2 * core, place - 1 + 2 * core, place + 2 - 4 * odd)
    ):
        mask_ref[8 + at : 9 + at, :] = jnp.where(tile == (reader & (TILES - 1)), 1.0, 0.0)
    mask_ref[12:16, :] = jnp.zeros((4, 128), F32)
    tile = lax.broadcasted_iota(jnp.int32, (TILES, 128), 0)
    asked = jnp.zeros((TILES, 128), F32)
    for part in range(OFFSETS):
        if part != REACH:
            reader = (place + part - REACH) & (TILES - 1)
            asked = jnp.where(tile == reader, blocks_ref[part].astype(F32), asked)
    lane = lax.broadcasted_iota(jnp.int32, (TILES, 128), 1)
    asked_ref[...] = jnp.where(lane == ASK_LANE, asked, 0.0)
    for copy in copies[9:]:
        copy.wait()


def interpolate_kernel(
    whole, behind, pair, own, across, ahead, high_ref, low_ref, factor_ref, row_ref, mask_ref,
    out_ref, neg_ref, pad_ref,
):
    high, low = high_ref[...], low_ref[...]
    second_core = mask_ref[5:6, :] > 0.5
    for n in range(2):
        pieces = []
        for part, source in enumerate((behind, pair, own, across, ahead)):
            if whole and part == 1:
                flat = source.reshape(2 * FULL, BLOCK)
                blocks = [
                    jnp.where(
                        second_core,
                        flat[pl.ds(2 * block + n, LEVELS, stride=4), :],
                        flat[pl.ds(FULL + 2 * block + n, LEVELS, stride=4), :],
                    )
                    for block in range(2)
                ]
                piece = jnp.where(mask_ref[part : part + 1, :] > 0.5, blocks[1], blocks[0])
            elif whole or part == 2:
                flat = (source.at[0] if whole and part == 2 else source).reshape(FULL, BLOCK)
                piece = jnp.where(
                    mask_ref[part : part + 1, :] > 0.5,
                    flat[pl.ds(2 + n, LEVELS, stride=4), :],
                    flat[pl.ds(n, LEVELS, stride=4), :],
                )
            elif part == 1:
                piece = jnp.where(
                    second_core,
                    source[pl.ds(n, LEVELS, stride=2), :],
                    source[pl.ds(HALF + n, LEVELS, stride=2), :],
                )
            else:
                piece = source[pl.ds(n, LEVELS, stride=2), :]
            pieces.append(piece)
        first, second = two_parts(jnp.concatenate(pieces, axis=1))
        pad_ref[n, 0:8, :] = jnp.zeros((8, TILE), F32)
        pad_ref[n, 144:152, :] = jnp.zeros((8, TILE), F32)
        pad_ref[n, 8 : 8 + LEVELS, :] = (
            jnp.dot(second, high, preferred_element_type=F32)
            + jnp.dot(first, low, preferred_element_type=F32)
        ) + jnp.dot(first, high, preferred_element_type=F32)
    total = [jnp.zeros((LEVELS, TILE), F32), jnp.zeros((LEVELS, TILE), F32)]
    for delta in range(-3, 5):
        factor = factor_ref[delta + 3]
        for n in range(2):
            total[n] = total[n] + factor * pad_ref[n, 8 + delta : 8 + delta + LEVELS, :]
    out_ref[0] = total[0]
    out_ref[1] = total[1]
    negative = jnp.minimum(total[0], 0.0) + jnp.minimum(total[1], 0.0)
    share = jnp.broadcast_to(row_ref[2:3, :] + row_ref[3:4, :], (8, TILE))
    for copy in range(4):
        neg_ref[copy, 136:PAD, :] = share
        neg_ref[copy, 0:LEVELS, :] = negative


def send_kernel(mixed_ref, parts_ref, send_ref, row_ref, asked_ref, kept_ref, out_ref, x_ref):
    all_parts = (parts_ref[0] + parts_ref[1]) + (parts_ref[2] + parts_ref[3])
    deficit = all_parts[0:LEVELS, :]
    whole = all_parts[LEVELS : LEVELS + 1, :]
    remap = row_ref[1:2, :]
    x_ref[256:384, :] = jnp.zeros((128, TILE), F32)
    for n in range(2):
        fixed = jnp.maximum(mixed_ref[n], 0.0) + (row_ref[2 + n : 3 + n, :] / whole) * deficit
        kept_ref[n] = (1.0 - remap) * fixed
        moved = remap * fixed
        x_ref[n * 128 : n * 128 + 128, :] = moved[0:128, :]
        x_ref[256 + 16 * n : 256 + 16 * n + 9, :] = moved[128:LEVELS, :]
    x_ref[256 + CELL_LANE : 257 + CELL_LANE, :] = row_ref[0:1, :]
    send = send_ref[...]
    dims = (((1,), (1,)), ((), ()))
    first, second = two_parts(x_ref[...])
    result = lax.dot_general(send, second, dims, preferred_element_type=F32)
    result = result + lax.dot_general(send, first, dims, preferred_element_type=F32)
    rest = asked_ref[...]
    for slot in range(SLOTS):
        rows = result[slot * TILES : (slot + 1) * TILES, :]
        for n in range(2):
            out_ref[pl.ds(2 * slot + n, TILES, stride=ROWS), :] = rows[:, n * 128 : n * 128 + 128]
        tail = rows[:, 256:384]
        if slot:
            tail = pltpu.roll(tail, 32 * slot, axis=1)
        rest = rest + tail
    out_ref[pl.ds(8, TILES, stride=ROWS), :] = rest


def landed(got_ref):
    rest = got_ref[pl.ds(8, TILES, stride=ROWS), :].T
    column = (lax.broadcasted_iota(jnp.int32, (TILE, TILES), 0) + 1).astype(F32)
    sums = [None, None]
    tails = [None, None]
    for slot in range(SLOTS):
        cell = rest[32 * slot + CELL_LANE : 32 * slot + CELL_LANE + 1, :]
        landing = jnp.where(column == cell, 1.0, 0.0).astype(BF16)
        for n in range(2):
            for piece in two_parts(got_ref[pl.ds(2 * slot + n, TILES, stride=ROWS), :]):
                term = jnp.dot(landing, piece, preferred_element_type=F32)
                sums[n] = term if sums[n] is None else sums[n] + term
            tail = rest[32 * slot + 16 * n : 32 * slot + 16 * n + 16, :]
            for piece in two_parts(tail):
                term = lax.dot_general(
                    piece, landing, (((1,), (1,)), ((), ())), preferred_element_type=F32
                )
                tails[n] = term if tails[n] is None else tails[n] + term
    tails = [value[0 : LEVELS - 128, :] for value in tails]
    return [value.T for value in sums], tails, rest[ASK_LANE : ASK_LANE + 1, :]


def land_kernel(kept_ref, got_ref, out_ref):
    sums, tails, _ = landed(got_ref)
    flat = out_ref.reshape(FULL, BLOCK)
    for n in range(2):
        upper = kept_ref[n, 0:128, :] + sums[n]
        lower = kept_ref[n, 128:LEVELS, :] + tails[n]
        for block in range(2):
            lanes = slice(block * BLOCK, (block + 1) * BLOCK)
            flat[pl.ds(2 * block + n, 128, stride=4), :] = upper[:, lanes]
            flat[pl.ds(512 + 2 * block + n, LEVELS - 128, stride=4), :] = lower[:, lanes]


def land_and_select_kernel(
    kept_ref, got_ref, mask_ref, out_ref, behind_ref, pair_ref, across_ref, ahead_ref
):
    sums, tails, asked = landed(got_ref)
    flat = out_ref.reshape(FULL, BLOCK)
    wanted = jnp.sum(mask_ref[8:16, :] * asked, axis=1, keepdims=True)
    asks = [wanted[at : at + 1, :] > 0.5 for at in range(4)]
    for n in range(2):
        for begin, count, values in ((0, 128, sums[n]), (128, LEVELS - 128, tails[n])):
            value = kept_ref[n, begin : begin + count, :] + values
            left, right = value[:, 0:BLOCK], value[:, BLOCK:TILE]
            flat[pl.ds(4 * begin + n, count, stride=4), :] = left
            flat[pl.ds(4 * begin + 2 + n, count, stride=4), :] = right
            for ask, ref in zip(asks, (behind_ref, pair_ref, across_ref, ahead_ref)):
                chosen = jnp.where(ask, right, left)
                ref[pl.ds(2 * begin + n, count, stride=2), :] = chosen
                if ref is pair_ref:
                    ref[pl.ds(HALF + 2 * begin + n, count, stride=2), :] = chosen


def cost(flops, moved):
    return pl.CostEstimate(flops=flops, bytes_accessed=moved, transcendentals=0)


def shards(
    tracers,
    dep_frac,
    vert_frac,
    vert_base,
    dep_blocks,
    dep_slot,
    dep_off,
    remap_share,
    remap_target,
    species_share,
):
    params = pltpu.CompilerParams(vmem_limit_bytes=48 * 1024 * 1024)
    shape = jax.ShapeDtypeStruct
    own = tracers.reshape(2, LEVELS, 2, BLOCK).transpose(1, 2, 0, 3).reshape(LEVELS, 4, BLOCK)
    to_behind, to_across, to_ahead = own, own, own
    high, low, factor, send, row, mask, asked, doubled = pl.pallas_call(
        prepare_kernel,
        name="prepare",
        out_shape=(
            shape((SOURCE, TILE), BF16),
            shape((SOURCE, TILE), BF16),
            shape((8, LEVELS, TILE), F32),
            shape((SLOTS * TILES, TILE), BF16),
            shape((8, TILE), F32),
            shape((16, 128), F32),
            shape((TILES, 128), F32),
            shape((2, LEVELS, 4, BLOCK), F32),
        ),
        in_specs=[pl.BlockSpec(memory_space=pltpu.MemorySpace.HBM)] * 10,
        out_specs=(VMEM,) * 8,
        scratch_shapes=[
            pltpu.VMEM((2, TILE), F32),
            pltpu.VMEM((TILE,), jnp.int32),
            pltpu.VMEM((TILE,), jnp.int32),
            pltpu.VMEM((TILE,), jnp.int32),
            pltpu.VMEM((TILE,), F32),
            pltpu.SMEM((OFFSETS,), jnp.int32),
            pltpu.SMEM((2,), F32),
            pltpu.VMEM((LEVELS, TILE), F32),
            pltpu.VMEM((LEVELS, TILE), jnp.int32),
            pltpu.SemaphoreType.DMA((11,)),
        ],
        compiler_params=params,
        cost_estimate=cost(40_000_000, 2_000_000),
    )(
        *[
            pltpu.with_memory_space_constraint(value, pltpu.MemorySpace.HBM)
            for value in (
                dep_frac, dep_slot, dep_off, remap_target, remap_share, dep_blocks.reshape(OFFSETS),
                species_share, vert_frac, vert_base, own,
            )
        ]
    )

    def interpolate(whole, *sources):
        return pl.pallas_call(
            functools.partial(interpolate_kernel, whole),
            name="interpolate",
            out_shape=(shape((2, LEVELS, TILE), F32), shape((4, PAD, TILE), F32)),
            in_specs=[VMEM] * 10,
            out_specs=(VMEM,) * 2,
            scratch_shapes=[pltpu.VMEM((2, 152, TILE), F32)],
            compiler_params=params,
            cost_estimate=cost(400_000_000, 3_000_000),
        )(*sources, high, low, factor, row, mask)

    dispatch = pl.pallas_call(
        send_kernel,
        name="dispatch",
        out_shape=(shape((2, LEVELS, TILE), F32), shape((TILES * ROWS, 128), F32)),
        in_specs=[VMEM] * 5,
        out_specs=(VMEM,) * 2,
        scratch_shapes=[pltpu.VMEM((384, TILE), F32)],
        compiler_params=params,
        cost_estimate=cost(200_000_000, 2_000_000),
    )
    land = pl.pallas_call(
        land_kernel,
        name="land",
        out_shape=shape((LEVELS, 4, BLOCK), F32),
        in_specs=[VMEM] * 2,
        out_specs=VMEM,
        compiler_params=params,
        cost_estimate=cost(200_000_000, 1_500_000),
    )
    land_and_select = pl.pallas_call(
        land_and_select_kernel,
        name="land_and_select",
        out_shape=(
            shape((LEVELS, 4, BLOCK), F32),
            shape((HALF, 128), F32),
            shape((2 * HALF, 128), F32),
            shape((HALF, 128), F32),
            shape((HALF, 128), F32),
        ),
        in_specs=[VMEM] * 3,
        out_specs=(VMEM,) * 5,
        compiler_params=params,
        cost_estimate=cost(200_000_000, 2_500_000),
    )
    for step_index in range(STEPS):
        behind = swap_chips(to_behind, 1)
        across = swap_across(to_across)
        ahead = swap_chips(to_ahead, 0)
        if step_index == 0:
            pair, own = swap_cores(doubled), doubled
        else:
            pair = swap_cores(to_pair.reshape(2, HALF, BLOCK)).reshape(2 * HALF, BLOCK)
        mixed, negative = interpolate(step_index == 0, behind, pair, own, across, ahead)
        parts = lax.all_to_all(negative, "trc", split_axis=0, concat_axis=0, tiled=True)
        kept, outgoing = dispatch(mixed, parts, send, row, asked)
        arrived = lax.all_to_all(
            outgoing.reshape(TILES, 1, ROWS * 128), "cols", split_axis=0, concat_axis=0, tiled=True
        ).reshape(TILES * ROWS, 128)
        if step_index + 1 < STEPS:
            own, to_behind, to_pair, to_across, to_ahead = land_and_select(kept, arrived, mask)
        else:
            own = land(kept, arrived)
    out = own.reshape(LEVELS, 2, 2, BLOCK).transpose(2, 0, 1, 3)
    return out.reshape(2, LEVELS, TILE)


def solution(mesh):
    return jax.shard_map(
        shards,
        mesh=mesh,
        in_specs=(
            P("trc", None, "cols"),
            P(None, "cols"),
            P(None, "cols"),
            P(None, "cols"),
            P("cols", None, None),
            P("cols"),
            P("cols"),
            P("cols"),
            P("cols"),
            P("trc"),
        ),
        out_specs=P("trc", None, "cols"),
        check_vma=False,
    )
```

```python
import functools

import jax
import jax.numpy as jnp
from jax import lax
from jax.experimental import pallas as pl
from jax.experimental.pallas import tpu as pltpu
from jax.sharding import PartitionSpec as P

BLOCK = 128
REACH = 2
STEPS = 2
LEVELS = 137
TILE = 256
TILES = 128
SLOTS = 4
OFFSETS = 2 * REACH + 1
SOURCE = OFFSETS * BLOCK
ROWS = 9
PAD = 144
HALF = 280
FULL = 4 * LEVELS
CELL_LANE = 9
ASK_LANE = 10
VMEM = pl.BlockSpec(memory_space=pltpu.VMEM)
F32 = jnp.float32
BF16 = jnp.bfloat16


def swap_chips(value, low):
    pairs = []
    for chip in range(low, TILES // 2 + low, 2):
        for core in range(2):
            here, there = (2 * chip + core) % TILES, (2 * chip + 2 + core) % TILES
            pairs += [(here, there), (there, here)]
    return lax.ppermute(value, "cols", sorted(pairs))


def swap_across(value):
    pairs = [(s, (s + 1) % TILES if s % 2 else (s - 1) % TILES) for s in range(TILES)]
    return lax.ppermute(value, "cols", pairs)


def swap_cores(value):
    groups = [[2 * chip, 2 * chip + 1] for chip in range(TILES // 2)]
    return lax.all_to_all(
        value, "cols", split_axis=0, concat_axis=0, tiled=True, axis_index_groups=groups
    )


def cubic_weights(fraction):
    return (
        -fraction * (fraction - 1.0) * (fraction - 2.0) / 6.0,
        (fraction + 1.0) * (fraction - 1.0) * (fraction - 2.0) / 2.0,
        -(fraction + 1.0) * fraction * (fraction - 2.0) / 2.0,
        (fraction + 1.0) * fraction * (fraction - 1.0) / 6.0,
    )


def two_parts(value):
    high = value.astype(BF16)
    return high, (value - high.astype(F32)).astype(BF16)


def pick(index, choices):
    value = jnp.where(index == 1, choices[1], choices[0])
    value = jnp.where(index == 2, choices[2], value)
    return jnp.where(index == 3, choices[3], value)


def prepare_kernel(
    frac_in, slot_in, off_in, target_in, remap_in, blocks_in, share_in, vert_in, base_in, own_in,
    high_ref, low_ref, factor_ref, send_ref, row_ref, mask_ref, asked_ref, own_ref,
    frac_ref, slot_ref, off_ref, target_ref, remap_ref, blocks_ref, share_ref, vert_ref, base_ref, sems,
):
    arrays = (
        frac_in, slot_in, off_in, target_in, remap_in, blocks_in, share_in, vert_in, base_in,
        own_in, own_in,
    )
    places = (
        frac_ref, slot_ref, off_ref, target_ref, remap_ref, blocks_ref, share_ref, vert_ref, base_ref,
        own_ref.at[0], own_ref.at[1],
    )
    copies = [
        pltpu.make_async_copy(array, there, sems.at[at])
        for at, (array, there) in enumerate(zip(arrays, places))
    ]
    for copy in copies:
        copy.start()
    for copy in copies[:9]:
        copy.wait()
    place = lax.axis_index("cols")
    core = place & 1
    odd = (place >> 1) & 1
    lon = cubic_weights(frac_ref[0:1, :])
    lat = cubic_weights(frac_ref[1:2, :])
    entry = slot_ref[...].reshape(1, TILE)
    turned = jnp.where((entry & 1) == 1, 1 - core, odd)
    entry = jnp.where(turned == 1, OFFSETS - 1 - entry, entry)
    first = entry * BLOCK + off_ref[...].reshape(1, TILE)
    for part in range(OFFSETS):
        row = lax.broadcasted_iota(jnp.int32, (BLOCK, TILE), 0) + part * BLOCK
        away = row - first
        column = away & 15
        inside = (away >= 0) & (away < 64) & (column < 4)
        weight = jnp.where(inside, pick(away >> 4, lat) * pick(column, lon), 0.0)
        high, low = two_parts(weight)
        high_ref[part * BLOCK : (part + 1) * BLOCK, :] = high
        low_ref[part * BLOCK : (part + 1) * BLOCK, :] = low
    vert = cubic_weights(vert_ref[...])
    away = base_ref[...] - lax.broadcasted_iota(jnp.int32, (LEVELS, TILE), 0)
    same = [away == delta for delta in range(-3, 2)]
    for delta in range(-3, 5):
        factor = jnp.zeros((LEVELS, TILE), F32)
        for tap in range(4):
            if -3 <= delta - tap <= 1:
                factor = jnp.where(same[delta - tap + 3], vert[tap], factor)
        factor_ref[delta + 3] = factor
    target = target_ref[...].reshape(1, TILE)
    owner = target >> 8
    hit = lax.broadcasted_iota(jnp.int32, (TILES, TILE), 0) == owner
    earlier = lax.broadcasted_iota(jnp.int32, (TILE, TILE), 0) < lax.broadcasted_iota(
        jnp.int32, (TILE, TILE), 1
    )
    one_hot = jnp.where(hit, 1.0, 0.0)
    rank = jnp.dot(
        one_hot.astype(BF16),
        jnp.where(earlier, 1.0, 0.0).astype(BF16),
        preferred_element_type=F32,
    )
    for slot in range(SLOTS):
        chosen = jnp.where(rank == slot, one_hot, 0.0)
        send_ref[slot * TILES : (slot + 1) * TILES, :] = chosen.astype(BF16)
    row_ref[0:1, :] = ((target & (TILE - 1)) + 1).astype(F32)
    row_ref[1:2, :] = remap_ref[...].reshape(1, TILE)
    row_ref[2:3, :] = jnp.full((1, TILE), share_ref[0], F32)
    row_ref[3:4, :] = jnp.full((1, TILE), share_ref[1], F32)
    row_ref[4:8, :] = jnp.zeros((4, TILE), F32)
    marks = [blocks_ref[at] for at in (4 * odd, 3 - 2 * core, 2, 1 + 2 * core, 4 - 4 * odd)] + [core]
    for at, mark in enumerate(marks):
        mask_ref[at : at + 1, :] = jnp.full((1, 128), mark, jnp.int32).astype(F32)
    mask_ref[6:8, :] = jnp.zeros((2, 128), F32)
    tile = lax.broadcasted_iota(jnp.int32, (1, 128), 1)
    for at, reader in enumerate(
        (place - 2 + 4 * odd, place + 1 - 2 * core, place - 1 + 2 * core, place + 2 - 4 * odd)
    ):
        mask_ref[8 + at : 9 + at, :] = jnp.where(tile == (reader & (TILES - 1)), 1.0, 0.0)
    mask_ref[12:16, :] = jnp.zeros((4, 128), F32)
    tile = lax.broadcasted_iota(jnp.int32, (TILES, 128), 0)
    asked = jnp.zeros((TILES, 128), F32)
    for part in range(OFFSETS):
        if part != REACH:
            reader = (place + part - REACH) & (TILES - 1)
            asked = jnp.where(tile == reader, blocks_ref[part].astype(F32), asked)
    lane = lax.broadcasted_iota(jnp.int32, (TILES, 128), 1)
    asked_ref[...] = jnp.where(lane == ASK_LANE, asked, 0.0)
    for copy in copies[9:]:
        copy.wait()


def interpolate_kernel(
    whole, s0, s1, s2, s3, s4, high_ref, low_ref, factor_ref, row_ref, mask_ref,
    out_ref, neg_ref, pad_ref,
):
    high, low = high_ref[...], low_ref[...]
    second_core = mask_ref[5:6, :] > 0.5
    for n in range(2):
        pieces = []
        for part, source in enumerate((s2, s3, s4, s0, s1) if whole else (s0, s1, s2, s3, s4)):
            if whole and part == 1:
                flat = source.reshape(2 * FULL, BLOCK)
                blocks = [
                    jnp.where(
                        second_core,
                        flat[pl.ds(2 * block + n, LEVELS, stride=4), :],
                        flat[pl.ds(FULL + 2 * block + n, LEVELS, stride=4), :],
                    )
                    for block in range(2)
                ]
                piece = jnp.where(mask_ref[part : part + 1, :] > 0.5, blocks[1], blocks[0])
            elif whole or part == 2:
                flat = (source.at[0] if whole and part == 2 else source).reshape(FULL, BLOCK)
                piece = jnp.where(
                    mask_ref[part : part + 1, :] > 0.5,
                    flat[pl.ds(2 + n, LEVELS, stride=4), :],
                    flat[pl.ds(n, LEVELS, stride=4), :],
                )
            elif part == 1:
                piece = jnp.where(
                    second_core,
                    source[pl.ds(n, LEVELS, stride=2), :],
                    source[pl.ds(HALF + n, LEVELS, stride=2), :],
                )
            else:
                piece = source[pl.ds(n, LEVELS, stride=2), :]
            pieces.append(piece)
        first, second = two_parts(jnp.concatenate(pieces, axis=1))
        pad_ref[n, 0:8, :] = jnp.zeros((8, TILE), F32)
        pad_ref[n, 144:152, :] = jnp.zeros((8, TILE), F32)
        pad_ref[n, 8 : 8 + LEVELS, :] = (
            jnp.dot(second, high, preferred_element_type=F32)
            + jnp.dot(first, low, preferred_element_type=F32)
        ) + jnp.dot(first, high, preferred_element_type=F32)
    total = [jnp.zeros((LEVELS, TILE), F32), jnp.zeros((LEVELS, TILE), F32)]
    for delta in range(-3, 5):
        factor = factor_ref[delta + 3]
        for n in range(2):
            total[n] = total[n] + factor * pad_ref[n, 8 + delta : 8 + delta + LEVELS, :]
    out_ref[0] = total[0]
    out_ref[1] = total[1]
    negative = jnp.minimum(total[0], 0.0) + jnp.minimum(total[1], 0.0)
    share = jnp.broadcast_to(row_ref[2:3, :] + row_ref[3:4, :], (8, TILE))
    for copy in range(4):
        neg_ref[copy, 136:PAD, :] = share
        neg_ref[copy, 0:LEVELS, :] = negative


def send_kernel(mixed_ref, parts_ref, send_ref, row_ref, asked_ref, kept_ref, out_ref, x_ref):
    all_parts = (parts_ref[0] + parts_ref[1]) + (parts_ref[2] + parts_ref[3])
    deficit = all_parts[0:LEVELS, :]
    whole = all_parts[LEVELS : LEVELS + 1, :]
    remap = row_ref[1:2, :]
    x_ref[256:384, :] = jnp.zeros((128, TILE), F32)
    for n in range(2):
        fixed = jnp.maximum(mixed_ref[n], 0.0) + (row_ref[2 + n : 3 + n, :] / whole) * deficit
        kept_ref[n] = (1.0 - remap) * fixed
        moved = remap * fixed
        x_ref[n * 128 : n * 128 + 128, :] = moved[0:128, :]
        x_ref[256 + 16 * n : 256 + 16 * n + 9, :] = moved[128:LEVELS, :]
    x_ref[256 + CELL_LANE : 257 + CELL_LANE, :] = row_ref[0:1, :]
    send = send_ref[...]
    dims = (((1,), (1,)), ((), ()))
    first, second = two_parts(x_ref[...])
    result = lax.dot_general(send, second, dims, preferred_element_type=F32)
    result = result + lax.dot_general(send, first, dims, preferred_element_type=F32)
    rest = asked_ref[...]
    for slot in range(SLOTS):
        rows = result[slot * TILES : (slot + 1) * TILES, :]
        for n in range(2):
            out_ref[pl.ds(2 * slot + n, TILES, stride=ROWS), :] = rows[:, n * 128 : n * 128 + 128]
        tail = rows[:, 256:384]
        if slot:
            tail = pltpu.roll(tail, 32 * slot, axis=1)
        rest = rest + tail
    out_ref[pl.ds(8, TILES, stride=ROWS), :] = rest


def landed(got_ref):
    rest = got_ref[pl.ds(8, TILES, stride=ROWS), :].T
    column = (lax.broadcasted_iota(jnp.int32, (TILE, TILES), 0) + 1).astype(F32)
    sums = [None, None]
    tails = [None, None]
    for slot in range(SLOTS):
        cell = rest[32 * slot + CELL_LANE : 32 * slot + CELL_LANE + 1, :]
        landing = jnp.where(column == cell, 1.0, 0.0).astype(BF16)
        for n in range(2):
            for piece in two_parts(got_ref[pl.ds(2 * slot + n, TILES, stride=ROWS), :]):
                term = jnp.dot(landing, piece, preferred_element_type=F32)
                sums[n] = term if sums[n] is None else sums[n] + term
            tail = rest[32 * slot + 16 * n : 32 * slot + 16 * n + 16, :]
            for piece in two_parts(tail):
                term = lax.dot_general(
                    piece, landing, (((1,), (1,)), ((), ())), preferred_element_type=F32
                )
                tails[n] = term if tails[n] is None else tails[n] + term
    tails = [value[0 : LEVELS - 128, :] for value in tails]
    return [value.T for value in sums], tails, rest[ASK_LANE : ASK_LANE + 1, :]


def land_kernel(kept_ref, got_ref, out_ref):
    sums, tails, _ = landed(got_ref)
    flat = out_ref.reshape(FULL, BLOCK)
    for n in range(2):
        upper = kept_ref[n, 0:128, :] + sums[n]
        lower = kept_ref[n, 128:LEVELS, :] + tails[n]
        for block in range(2):
            lanes = slice(block * BLOCK, (block + 1) * BLOCK)
            flat[pl.ds(2 * block + n, 128, stride=4), :] = upper[:, lanes]
            flat[pl.ds(512 + 2 * block + n, LEVELS - 128, stride=4), :] = lower[:, lanes]


def land_and_select_kernel(
    kept_ref, got_ref, mask_ref, out_ref, behind_ref, pair_ref, across_ref, ahead_ref
):
    sums, tails, asked = landed(got_ref)
    flat = out_ref.reshape(FULL, BLOCK)
    wanted = jnp.sum(mask_ref[8:16, :] * asked, axis=1, keepdims=True)
    asks = [wanted[at : at + 1, :] > 0.5 for at in range(4)]
    for n in range(2):
        for begin, count, values in ((0, 128, sums[n]), (128, LEVELS - 128, tails[n])):
            value = kept_ref[n, begin : begin + count, :] + values
            left, right = value[:, 0:BLOCK], value[:, BLOCK:TILE]
            flat[pl.ds(4 * begin + n, count, stride=4), :] = left
            flat[pl.ds(4 * begin + 2 + n, count, stride=4), :] = right
            for ask, ref in zip(asks, (behind_ref, pair_ref, across_ref, ahead_ref)):
                chosen = jnp.where(ask, right, left)
                ref[pl.ds(2 * begin + n, count, stride=2), :] = chosen
                if ref is pair_ref:
                    ref[pl.ds(HALF + 2 * begin + n, count, stride=2), :] = chosen


def cost(flops, moved):
    return pl.CostEstimate(flops=flops, bytes_accessed=moved, transcendentals=0)


def shards(
    tracers,
    dep_frac,
    vert_frac,
    vert_base,
    dep_blocks,
    dep_slot,
    dep_off,
    remap_share,
    remap_target,
    species_share,
):
    params = pltpu.CompilerParams(vmem_limit_bytes=48 * 1024 * 1024)
    shape = jax.ShapeDtypeStruct
    own = tracers.reshape(2, LEVELS, 2, BLOCK).transpose(1, 2, 0, 3).reshape(LEVELS, 4, BLOCK)
    to_behind, to_across, to_ahead = own, own, own
    high, low, factor, send, row, mask, asked, doubled = pl.pallas_call(
        prepare_kernel,
        name="prepare",
        out_shape=(
            shape((SOURCE, TILE), BF16),
            shape((SOURCE, TILE), BF16),
            shape((8, LEVELS, TILE), F32),
            shape((SLOTS * TILES, TILE), BF16),
            shape((8, TILE), F32),
            shape((16, 128), F32),
            shape((TILES, 128), F32),
            shape((2, LEVELS, 4, BLOCK), F32),
        ),
        in_specs=[pl.BlockSpec(memory_space=pltpu.MemorySpace.HBM)] * 10,
        out_specs=(VMEM,) * 8,
        scratch_shapes=[
            pltpu.VMEM((2, TILE), F32),
            pltpu.VMEM((TILE,), jnp.int32),
            pltpu.VMEM((TILE,), jnp.int32),
            pltpu.VMEM((TILE,), jnp.int32),
            pltpu.VMEM((TILE,), F32),
            pltpu.SMEM((OFFSETS,), jnp.int32),
            pltpu.SMEM((2,), F32),
            pltpu.VMEM((LEVELS, TILE), F32),
            pltpu.VMEM((LEVELS, TILE), jnp.int32),
            pltpu.SemaphoreType.DMA((11,)),
        ],
        compiler_params=params,
        cost_estimate=cost(40_000_000, 2_000_000),
    )(
        *[
            pltpu.with_memory_space_constraint(value, pltpu.MemorySpace.HBM)
            for value in (
                dep_frac, dep_slot, dep_off, remap_target, remap_share, dep_blocks.reshape(OFFSETS),
                species_share, vert_frac, vert_base, own,
            )
        ]
    )

    def interpolate(whole, *sources):
        return pl.pallas_call(
            functools.partial(interpolate_kernel, whole),
            name="interpolate",
            out_shape=(shape((2, LEVELS, TILE), F32), shape((4, PAD, TILE), F32)),
            in_specs=[VMEM] * 10,
            out_specs=(VMEM,) * 2,
            scratch_shapes=[pltpu.VMEM((2, 152, TILE), F32)],
            compiler_params=params,
            cost_estimate=cost(400_000_000, 3_000_000),
        )(*sources, high, low, factor, row, mask)

    dispatch = pl.pallas_call(
        send_kernel,
        name="dispatch",
        out_shape=(shape((2, LEVELS, TILE), F32), shape((TILES * ROWS, 128), F32)),
        in_specs=[VMEM] * 5,
        out_specs=(VMEM,) * 2,
        scratch_shapes=[pltpu.VMEM((384, TILE), F32)],
        compiler_params=params,
        cost_estimate=cost(200_000_000, 2_000_000),
    )
    land = pl.pallas_call(
        land_kernel,
        name="land",
        out_shape=shape((LEVELS, 4, BLOCK), F32),
        in_specs=[VMEM] * 2,
        out_specs=VMEM,
        compiler_params=params,
        cost_estimate=cost(200_000_000, 1_500_000),
    )
    land_and_select = pl.pallas_call(
        land_and_select_kernel,
        name="land_and_select",
        out_shape=(
            shape((LEVELS, 4, BLOCK), F32),
            shape((HALF, 128), F32),
            shape((2 * HALF, 128), F32),
            shape((HALF, 128), F32),
            shape((HALF, 128), F32),
        ),
        in_specs=[VMEM] * 3,
        out_specs=(VMEM,) * 5,
        compiler_params=params,
        cost_estimate=cost(200_000_000, 2_500_000),
    )
    for step_index in range(STEPS):
        behind = swap_chips(to_behind, 1)
        across = swap_across(to_across)
        ahead = swap_chips(to_ahead, 0)
        if step_index == 0:
            pair, own = swap_cores(doubled), doubled
        else:
            pair = swap_cores(to_pair.reshape(2, HALF, BLOCK)).reshape(2 * HALF, BLOCK)
        if step_index == 0:
            mixed, negative = interpolate(True, across, ahead, behind, pair, own)
        else:
            mixed, negative = interpolate(False, behind, pair, own, across, ahead)
        parts = lax.all_to_all(negative, "trc", split_axis=0, concat_axis=0, tiled=True)
        kept, outgoing = dispatch(mixed, parts, send, row, asked)
        arrived = lax.all_to_all(
            outgoing.reshape(TILES, 1, ROWS * 128), "cols", split_axis=0, concat_axis=0, tiled=True
        ).reshape(TILES * ROWS, 128)
        if step_index + 1 < STEPS:
            own, to_behind, to_pair, to_across, to_ahead = land_and_select(kept, arrived, mask)
        else:
            own = land(kept, arrived)
    out = own.reshape(LEVELS, 2, 2, BLOCK).transpose(2, 0, 1, 3)
    return out.reshape(2, LEVELS, TILE)


def solution(mesh):
    return jax.shard_map(
        shards,
        mesh=mesh,
        in_specs=(
            P("trc", None, "cols"),
            P(None, "cols"),
            P(None, "cols"),
            P(None, "cols"),
            P("cols", None, None),
            P("cols"),
            P("cols"),
            P("cols"),
            P("cols"),
            P("trc"),
        ),
        out_specs=P("trc", None, "cols"),
        check_vma=False,
    )
```

```python
import functools

import jax
import jax.numpy as jnp
from jax import lax
from jax.experimental import pallas as pl
from jax.experimental.pallas import tpu as pltpu
from jax.sharding import PartitionSpec as P

BLOCK = 128
REACH = 2
STEPS = 2
LEVELS = 137
TILE = 256
TILES = 128
SLOTS = 4
OFFSETS = 2 * REACH + 1
SOURCE = OFFSETS * BLOCK
ROWS = 9
PAD = 144
HALF = 280
FULL = 4 * LEVELS
CELL_LANE = 9
ASK_LANE = 10
VMEM = pl.BlockSpec(memory_space=pltpu.VMEM)
F32 = jnp.float32
BF16 = jnp.bfloat16


def swap_chips(value, low):
    pairs = []
    for chip in range(low, TILES // 2 + low, 2):
        for core in range(2):
            here, there = (2 * chip + core) % TILES, (2 * chip + 2 + core) % TILES
            pairs += [(here, there), (there, here)]
    return lax.ppermute(value, "cols", sorted(pairs))


def swap_across(value):
    pairs = [(s, (s + 1) % TILES if s % 2 else (s - 1) % TILES) for s in range(TILES)]
    return lax.ppermute(value, "cols", pairs)


def swap_pair(value):
    return lax.ppermute(value, "cols", [(s, s ^ 1) for s in range(TILES)])


def swap_cores(value):
    groups = [[2 * chip, 2 * chip + 1] for chip in range(TILES // 2)]
    return lax.all_to_all(
        value, "cols", split_axis=0, concat_axis=0, tiled=True, axis_index_groups=groups
    )


def cubic_weights(fraction):
    return (
        -fraction * (fraction - 1.0) * (fraction - 2.0) / 6.0,
        (fraction + 1.0) * (fraction - 1.0) * (fraction - 2.0) / 2.0,
        -(fraction + 1.0) * fraction * (fraction - 2.0) / 2.0,
        (fraction + 1.0) * fraction * (fraction - 1.0) / 6.0,
    )


def two_parts(value):
    high = value.astype(BF16)
    return high, (value - high.astype(F32)).astype(BF16)


def pick(index, choices):
    value = jnp.where(index == 1, choices[1], choices[0])
    value = jnp.where(index == 2, choices[2], value)
    return jnp.where(index == 3, choices[3], value)


def prepare_kernel(
    frac_in, slot_in, off_in, target_in, remap_in, blocks_in, share_in, vert_in, base_in, own_in,
    high_ref, low_ref, factor_ref, send_ref, row_ref, mask_ref, asked_ref, own_ref,
    frac_ref, slot_ref, off_ref, target_ref, remap_ref, blocks_ref, share_ref, vert_ref, base_ref, sems,
):
    arrays = (
        frac_in, slot_in, off_in, target_in, remap_in, blocks_in, share_in, vert_in, base_in,
        own_in,
    )
    places = (
        frac_ref, slot_ref, off_ref, target_ref, remap_ref, blocks_ref, share_ref, vert_ref, base_ref,
        own_ref,
    )
    copies = [
        pltpu.make_async_copy(array, there, sems.at[at])
        for at, (array, there) in enumerate(zip(arrays, places))
    ]
    for copy in copies:
        copy.start()
    for copy in copies[:7]:
        copy.wait()
    place = lax.axis_index("cols")
    core = place & 1
    odd = (place >> 1) & 1
    lon = cubic_weights(frac_ref[0:1, :])
    lat = cubic_weights(frac_ref[1:2, :])
    entry = slot_ref[...].reshape(1, TILE)
    turned = jnp.where((entry & 1) == 1, 1 - core, odd)
    entry = jnp.where(turned == 1, OFFSETS - 1 - entry, entry)
    first = entry * BLOCK + off_ref[...].reshape(1, TILE)
    for part in range(OFFSETS):
        row = lax.broadcasted_iota(jnp.int32, (BLOCK, TILE), 0) + part * BLOCK
        away = row - first
        column = away & 15
        inside = (away >= 0) & (away < 64) & (column < 4)
        weight = jnp.where(inside, pick(away >> 4, lat) * pick(column, lon), 0.0)
        high, low = two_parts(weight)
        high_ref[part * BLOCK : (part + 1) * BLOCK, :] = high
        low_ref[part * BLOCK : (part + 1) * BLOCK, :] = low
    for copy in copies[7:9]:
        copy.wait()
    vert = cubic_weights(vert_ref[...])
    away = base_ref[...] - lax.broadcasted_iota(jnp.int32, (LEVELS, TILE), 0)
    same = [away == delta for delta in range(-3, 2)]
    for delta in range(-3, 5):
        factor = jnp.zeros((LEVELS, TILE), F32)
        for tap in range(4):
            if -3 <= delta - tap <= 1:
                factor = jnp.where(same[delta - tap + 3], vert[tap], factor)
        factor_ref[delta + 3] = factor
    target = target_ref[...].reshape(1, TILE)
    owner = target >> 8
    hit = lax.broadcasted_iota(jnp.int32, (TILES, TILE), 0) == owner
    earlier = lax.broadcasted_iota(jnp.int32, (TILE, TILE), 0) < lax.broadcasted_iota(
        jnp.int32, (TILE, TILE), 1
    )
    one_hot = jnp.where(hit, 1.0, 0.0)
    rank = jnp.dot(
        one_hot.astype(BF16),
        jnp.where(earlier, 1.0, 0.0).astype(BF16),
        preferred_element_type=F32,
    )
    for slot in range(SLOTS):
        chosen = jnp.where(rank == slot, one_hot, 0.0)
        send_ref[slot * TILES : (slot + 1) * TILES, :] = chosen.astype(BF16)
    row_ref[0:1, :] = ((target & (TILE - 1)) + 1).astype(F32)
    row_ref[1:2, :] = remap_ref[...].reshape(1, TILE)
    row_ref[2:3, :] = jnp.full((1, TILE), share_ref[0], F32)
    row_ref[3:4, :] = jnp.full((1, TILE), share_ref[1], F32)
    row_ref[4:8, :] = jnp.zeros((4, TILE), F32)
    marks = [blocks_ref[at] for at in (4 * odd, 3 - 2 * core, 2, 1 + 2 * core, 4 - 4 * odd)] + [core]
    for at, mark in enumerate(marks):
        mask_ref[at : at + 1, :] = jnp.full((1, 128), mark, jnp.int32).astype(F32)
    mask_ref[6:8, :] = jnp.zeros((2, 128), F32)
    tile = lax.broadcasted_iota(jnp.int32, (1, 128), 1)
    for at, reader in enumerate(
        (place - 2 + 4 * odd, place + 1 - 2 * core, place - 1 + 2 * core, place + 2 - 4 * odd)
    ):
        mask_ref[8 + at : 9 + at, :] = jnp.where(tile == (reader & (TILES - 1)), 1.0, 0.0)
    mask_ref[12:16, :] = jnp.zeros((4, 128), F32)
    tile = lax.broadcasted_iota(jnp.int32, (TILES, 128), 0)
    asked = jnp.zeros((TILES, 128), F32)
    for part in range(OFFSETS):
        if part != REACH:
            reader = (place + part - REACH) & (TILES - 1)
            asked = jnp.where(tile == reader, blocks_ref[part].astype(F32), asked)
    lane = lax.broadcasted_iota(jnp.int32, (TILES, 128), 1)
    asked_ref[...] = jnp.where(lane == ASK_LANE, asked, 0.0)
    for copy in copies[9:]:
        copy.wait()


def interpolate_kernel(
    whole, s0, s1, s2, s3, s4, high_ref, low_ref, factor_ref, row_ref, mask_ref,
    out_ref, neg_ref, pad_ref,
):
    high, low = high_ref[...], low_ref[...]
    second_core = mask_ref[5:6, :] > 0.5
    for n in range(2):
        pieces = []
        for part, source in enumerate((s3, s0, s4, s1, s2) if whole else (s0, s1, s2, s3, s4)):
            if whole or part == 2:
                flat = source.reshape(FULL, BLOCK)
                piece = jnp.where(
                    mask_ref[part : part + 1, :] > 0.5,
                    flat[pl.ds(2 + n, LEVELS, stride=4), :],
                    flat[pl.ds(n, LEVELS, stride=4), :],
                )
            elif part == 1:
                piece = jnp.where(
                    second_core,
                    source[pl.ds(n, LEVELS, stride=2), :],
                    source[pl.ds(HALF + n, LEVELS, stride=2), :],
                )
            else:
                piece = source[pl.ds(n, LEVELS, stride=2), :]
            pieces.append(piece)
        first, second = two_parts(jnp.concatenate(pieces, axis=1))
        pad_ref[n, 0:8, :] = jnp.zeros((8, TILE), F32)
        pad_ref[n, 144:152, :] = jnp.zeros((8, TILE), F32)
        pad_ref[n, 8 : 8 + LEVELS, :] = (
            jnp.dot(second, high, preferred_element_type=F32)
            + jnp.dot(first, low, preferred_element_type=F32)
        ) + jnp.dot(first, high, preferred_element_type=F32)
    total = [jnp.zeros((LEVELS, TILE), F32), jnp.zeros((LEVELS, TILE), F32)]
    for delta in range(-3, 5):
        factor = factor_ref[delta + 3]
        for n in range(2):
            total[n] = total[n] + factor * pad_ref[n, 8 + delta : 8 + delta + LEVELS, :]
    out_ref[0] = total[0]
    out_ref[1] = total[1]
    negative = jnp.minimum(total[0], 0.0) + jnp.minimum(total[1], 0.0)
    share = jnp.broadcast_to(row_ref[2:3, :] + row_ref[3:4, :], (8, TILE))
    for copy in range(4):
        neg_ref[copy, 136:PAD, :] = share
        neg_ref[copy, 0:LEVELS, :] = negative


def send_kernel(mixed_ref, parts_ref, send_ref, row_ref, asked_ref, kept_ref, out_ref, x_ref):
    all_parts = (parts_ref[0] + parts_ref[1]) + (parts_ref[2] + parts_ref[3])
    deficit = all_parts[0:LEVELS, :]
    whole = all_parts[LEVELS : LEVELS + 1, :]
    remap = row_ref[1:2, :]
    x_ref[256:384, :] = jnp.zeros((128, TILE), F32)
    for n in range(2):
        fixed = jnp.maximum(mixed_ref[n], 0.0) + (row_ref[2 + n : 3 + n, :] / whole) * deficit
        kept_ref[n] = (1.0 - remap) * fixed
        moved = remap * fixed
        x_ref[n * 128 : n * 128 + 128, :] = moved[0:128, :]
        x_ref[256 + 16 * n : 256 + 16 * n + 9, :] = moved[128:LEVELS, :]
    x_ref[256 + CELL_LANE : 257 + CELL_LANE, :] = row_ref[0:1, :]
    send = send_ref[...]
    dims = (((1,), (1,)), ((), ()))
    first, second = two_parts(x_ref[...])
    result = lax.dot_general(send, second, dims, preferred_element_type=F32)
    result = result + lax.dot_general(send, first, dims, preferred_element_type=F32)
    rest = asked_ref[...]
    for slot in range(SLOTS):
        rows = result[slot * TILES : (slot + 1) * TILES, :]
        for n in range(2):
            out_ref[pl.ds(2 * slot + n, TILES, stride=ROWS), :] = rows[:, n * 128 : n * 128 + 128]
        tail = rows[:, 256:384]
        if slot:
            tail = pltpu.roll(tail, 32 * slot, axis=1)
        rest = rest + tail
    out_ref[pl.ds(8, TILES, stride=ROWS), :] = rest


def landed(got_ref):
    rest = got_ref[pl.ds(8, TILES, stride=ROWS), :].T
    column = (lax.broadcasted_iota(jnp.int32, (TILE, TILES), 0) + 1).astype(F32)
    sums = [None, None]
    tails = [None, None]
    for slot in range(SLOTS):
        cell = rest[32 * slot + CELL_LANE : 32 * slot + CELL_LANE + 1, :]
        landing = jnp.where(column == cell, 1.0, 0.0).astype(BF16)
        for n in range(2):
            for piece in two_parts(got_ref[pl.ds(2 * slot + n, TILES, stride=ROWS), :]):
                term = jnp.dot(landing, piece, preferred_element_type=F32)
                sums[n] = term if sums[n] is None else sums[n] + term
            tail = rest[32 * slot + 16 * n : 32 * slot + 16 * n + 16, :]
            for piece in two_parts(tail):
                term = lax.dot_general(
                    piece, landing, (((1,), (1,)), ((), ())), preferred_element_type=F32
                )
                tails[n] = term if tails[n] is None else tails[n] + term
    tails = [value[0 : LEVELS - 128, :] for value in tails]
    return [value.T for value in sums], tails, rest[ASK_LANE : ASK_LANE + 1, :]


def land_kernel(kept_ref, got_ref, out_ref):
    sums, tails, _ = landed(got_ref)
    flat = out_ref.reshape(FULL, BLOCK)
    for n in range(2):
        upper = kept_ref[n, 0:128, :] + sums[n]
        lower = kept_ref[n, 128:LEVELS, :] + tails[n]
        for block in range(2):
            lanes = slice(block * BLOCK, (block + 1) * BLOCK)
            flat[pl.ds(2 * block + n, 128, stride=4), :] = upper[:, lanes]
            flat[pl.ds(512 + 2 * block + n, LEVELS - 128, stride=4), :] = lower[:, lanes]


def land_and_select_kernel(
    kept_ref, got_ref, mask_ref, out_ref, behind_ref, pair_ref, across_ref, ahead_ref
):
    sums, tails, asked = landed(got_ref)
    flat = out_ref.reshape(FULL, BLOCK)
    wanted = jnp.sum(mask_ref[8:16, :] * asked, axis=1, keepdims=True)
    asks = [wanted[at : at + 1, :] > 0.5 for at in range(4)]
    for n in range(2):
        for begin, count, values in ((0, 128, sums[n]), (128, LEVELS - 128, tails[n])):
            value = kept_ref[n, begin : begin + count, :] + values
            left, right = value[:, 0:BLOCK], value[:, BLOCK:TILE]
            flat[pl.ds(4 * begin + n, count, stride=4), :] = left
            flat[pl.ds(4 * begin + 2 + n, count, stride=4), :] = right
            for ask, ref in zip(asks, (behind_ref, pair_ref, across_ref, ahead_ref)):
                chosen = jnp.where(ask, right, left)
                ref[pl.ds(2 * begin + n, count, stride=2), :] = chosen
                if ref is pair_ref:
                    ref[pl.ds(HALF + 2 * begin + n, count, stride=2), :] = chosen


def cost(flops, moved):
    return pl.CostEstimate(flops=flops, bytes_accessed=moved, transcendentals=0)


def shards(
    tracers,
    dep_frac,
    vert_frac,
    vert_base,
    dep_blocks,
    dep_slot,
    dep_off,
    remap_share,
    remap_target,
    species_share,
):
    params = pltpu.CompilerParams(vmem_limit_bytes=48 * 1024 * 1024)
    shape = jax.ShapeDtypeStruct
    own = tracers.reshape(2, LEVELS, 2, BLOCK).transpose(1, 2, 0, 3).reshape(LEVELS, 4, BLOCK)
    to_behind, to_across, to_ahead = own, own, own
    high, low, factor, send, row, mask, asked, first_own = pl.pallas_call(
        prepare_kernel,
        name="prepare",
        out_shape=(
            shape((SOURCE, TILE), BF16),
            shape((SOURCE, TILE), BF16),
            shape((8, LEVELS, TILE), F32),
            shape((SLOTS * TILES, TILE), BF16),
            shape((8, TILE), F32),
            shape((16, 128), F32),
            shape((TILES, 128), F32),
            shape((LEVELS, 4, BLOCK), F32),
        ),
        in_specs=[pl.BlockSpec(memory_space=pltpu.MemorySpace.HBM)] * 10,
        out_specs=(VMEM,) * 8,
        scratch_shapes=[
            pltpu.VMEM((2, TILE), F32),
            pltpu.VMEM((TILE,), jnp.int32),
            pltpu.VMEM((TILE,), jnp.int32),
            pltpu.VMEM((TILE,), jnp.int32),
            pltpu.VMEM((TILE,), F32),
            pltpu.SMEM((OFFSETS,), jnp.int32),
            pltpu.SMEM((2,), F32),
            pltpu.VMEM((LEVELS, TILE), F32),
            pltpu.VMEM((LEVELS, TILE), jnp.int32),
            pltpu.SemaphoreType.DMA((10,)),
        ],
        compiler_params=params,
        cost_estimate=cost(40_000_000, 2_000_000),
    )(
        *[
            pltpu.with_memory_space_constraint(value, pltpu.MemorySpace.HBM)
            for value in (
                dep_frac, dep_slot, dep_off, remap_target, remap_share, dep_blocks.reshape(OFFSETS),
                species_share, vert_frac, vert_base, own,
            )
        ]
    )

    def interpolate(whole, *sources):
        return pl.pallas_call(
            functools.partial(interpolate_kernel, whole),
            name="interpolate",
            out_shape=(shape((2, LEVELS, TILE), F32), shape((4, PAD, TILE), F32)),
            in_specs=[VMEM] * 10,
            out_specs=(VMEM,) * 2,
            scratch_shapes=[pltpu.VMEM((2, 152, TILE), F32)],
            compiler_params=params,
            cost_estimate=cost(400_000_000, 3_000_000),
        )(*sources, high, low, factor, row, mask)

    dispatch = pl.pallas_call(
        send_kernel,
        name="dispatch",
        out_shape=(shape((2, LEVELS, TILE), F32), shape((TILES * ROWS, 128), F32)),
        in_specs=[VMEM] * 5,
        out_specs=(VMEM,) * 2,
        scratch_shapes=[pltpu.VMEM((384, TILE), F32)],
        compiler_params=params,
        cost_estimate=cost(200_000_000, 2_000_000),
    )
    land = pl.pallas_call(
        land_kernel,
        name="land",
        out_shape=shape((LEVELS, 4, BLOCK), F32),
        in_specs=[VMEM] * 2,
        out_specs=VMEM,
        compiler_params=params,
        cost_estimate=cost(200_000_000, 1_500_000),
    )
    land_and_select = pl.pallas_call(
        land_and_select_kernel,
        name="land_and_select",
        out_shape=(
            shape((LEVELS, 4, BLOCK), F32),
            shape((HALF, 128), F32),
            shape((2 * HALF, 128), F32),
            shape((HALF, 128), F32),
            shape((HALF, 128), F32),
        ),
        in_specs=[VMEM] * 3,
        out_specs=(VMEM,) * 5,
        compiler_params=params,
        cost_estimate=cost(200_000_000, 2_500_000),
    )
    for step_index in range(STEPS):
        behind = swap_chips(to_behind, 1)
        across = swap_across(to_across)
        ahead = swap_chips(to_ahead, 0)
        if step_index == 0:
            pair, own = swap_pair(own), first_own
        else:
            pair = swap_cores(to_pair.reshape(2, HALF, BLOCK)).reshape(2 * HALF, BLOCK)
        if step_index == 0:
            mixed, negative = interpolate(True, pair, across, ahead, behind, own)
        else:
            mixed, negative = interpolate(False, behind, pair, own, across, ahead)
        parts = lax.all_to_all(negative, "trc", split_axis=0, concat_axis=0, tiled=True)
        kept, outgoing = dispatch(mixed, parts, send, row, asked)
        arrived = lax.all_to_all(
            outgoing.reshape(TILES, 1, ROWS * 128), "cols", split_axis=0, concat_axis=0, tiled=True
        ).reshape(TILES * ROWS, 128)
        if step_index + 1 < STEPS:
            own, to_behind, to_pair, to_across, to_ahead = land_and_select(kept, arrived, mask)
        else:
            own = land(kept, arrived)
    out = own.reshape(LEVELS, 2, 2, BLOCK).transpose(2, 0, 1, 3)
    return out.reshape(2, LEVELS, TILE)


def solution(mesh):
    return jax.shard_map(
        shards,
        mesh=mesh,
        in_specs=(
            P("trc", None, "cols"),
            P(None, "cols"),
            P(None, "cols"),
            P(None, "cols"),
            P("cols", None, None),
            P("cols"),
            P("cols"),
            P("cols"),
            P("cols"),
            P("trc"),
        ),
        out_specs=P("trc", None, "cols"),
        check_vma=False,
    )
```

```python
import functools

import jax
import jax.numpy as jnp
from jax import lax
from jax.experimental import pallas as pl
from jax.experimental.pallas import tpu as pltpu
from jax.sharding import PartitionSpec as P

BLOCK = 128
REACH = 2
STEPS = 2
LEVELS = 137
TILE = 256
TILES = 128
SLOTS = 4
OFFSETS = 2 * REACH + 1
SOURCE = OFFSETS * BLOCK
ROWS = 9
PAD = 144
HALF = 280
FULL = 4 * LEVELS
CELL_LANE = 9
ASK_LANE = 10
VMEM = pl.BlockSpec(memory_space=pltpu.VMEM)
F32 = jnp.float32
BF16 = jnp.bfloat16


def swap_chips(value, low):
    pairs = []
    for chip in range(low, TILES // 2 + low, 2):
        for core in range(2):
            here, there = (2 * chip + core) % TILES, (2 * chip + 2 + core) % TILES
            pairs += [(here, there), (there, here)]
    return lax.ppermute(value, "cols", sorted(pairs))


def swap_across(value):
    pairs = [(s, (s + 1) % TILES if s % 2 else (s - 1) % TILES) for s in range(TILES)]
    return lax.ppermute(value, "cols", pairs)


def swap_cores(value):
    groups = [[2 * chip, 2 * chip + 1] for chip in range(TILES // 2)]
    return lax.all_to_all(
        value, "cols", split_axis=0, concat_axis=0, tiled=True, axis_index_groups=groups
    )


def cubic_weights(fraction):
    return (
        -fraction * (fraction - 1.0) * (fraction - 2.0) / 6.0,
        (fraction + 1.0) * (fraction - 1.0) * (fraction - 2.0) / 2.0,
        -(fraction + 1.0) * fraction * (fraction - 2.0) / 2.0,
        (fraction + 1.0) * fraction * (fraction - 1.0) / 6.0,
    )


def two_parts(value):
    high = value.astype(BF16)
    return high, (value - high.astype(F32)).astype(BF16)


def pick(index, choices):
    value = jnp.where(index == 1, choices[1], choices[0])
    value = jnp.where(index == 2, choices[2], value)
    return jnp.where(index == 3, choices[3], value)


def prepare_kernel(
    frac_in, slot_in, off_in, target_in, remap_in, blocks_in, share_in, vert_in, base_in, own_in,
    high_ref, low_ref, factor_ref, send_ref, row_ref, mask_ref, asked_ref, own_ref,
    frac_ref, slot_ref, off_ref, target_ref, remap_ref, blocks_ref, share_ref, vert_ref, base_ref, sems,
):
    arrays = (
        frac_in, slot_in, off_in, target_in, remap_in, blocks_in, share_in, vert_in, base_in,
        own_in, own_in,
    )
    places = (
        frac_ref, slot_ref, off_ref, target_ref, remap_ref, blocks_ref, share_ref, vert_ref, base_ref,
        own_ref.at[0], own_ref.at[1],
    )
    copies = [
        pltpu.make_async_copy(array, there, sems.at[at])
        for at, (array, there) in enumerate(zip(arrays, places))
    ]
    for copy in copies:
        copy.start()
    for copy in copies[:9]:
        copy.wait()
    place = lax.axis_index("cols")
    core = place & 1
    odd = (place >> 1) & 1
    lon = cubic_weights(frac_ref[0:1, :])
    lat = cubic_weights(frac_ref[1:2, :])
    entry = slot_ref[...].reshape(1, TILE)
    turned = jnp.where((entry & 1) == 1, 1 - core, odd)
    entry = jnp.where(turned == 1, OFFSETS - 1 - entry, entry)
    first = entry * BLOCK + off_ref[...].reshape(1, TILE)
    for part in range(OFFSETS):
        row = lax.broadcasted_iota(jnp.int32, (BLOCK, TILE), 0) + part * BLOCK
        away = row - first
        column = away & 15
        inside = (away >= 0) & (away < 64) & (column < 4)
        weight = jnp.where(inside, pick(away >> 4, lat) * pick(column, lon), 0.0)
        high, low = two_parts(weight)
        high_ref[part * BLOCK : (part + 1) * BLOCK, :] = high
        low_ref[part * BLOCK : (part + 1) * BLOCK, :] = low
    vert = cubic_weights(vert_ref[...])
    away = base_ref[...] - lax.broadcasted_iota(jnp.int32, (LEVELS, TILE), 0)
    same = [away == delta for delta in range(-3, 2)]
    for delta in range(-3, 5):
        factor = jnp.zeros((LEVELS, TILE), F32)
        for tap in range(4):
            if -3 <= delta - tap <= 1:
                factor = jnp.where(same[delta - tap + 3], vert[tap], factor)
        factor_ref[delta + 3] = factor
    target = target_ref[...].reshape(1, TILE)
    owner = target >> 8
    hit = lax.broadcasted_iota(jnp.int32, (TILES, TILE), 0) == owner
    earlier = lax.broadcasted_iota(jnp.int32, (TILE, TILE), 0) < lax.broadcasted_iota(
        jnp.int32, (TILE, TILE), 1
    )
    one_hot = jnp.where(hit, 1.0, 0.0)
    rank = jnp.dot(
        one_hot.astype(BF16),
        jnp.where(earlier, 1.0, 0.0).astype(BF16),
        preferred_element_type=F32,
    )
    for slot in range(SLOTS):
        chosen = jnp.where(rank == slot, one_hot, 0.0)
        send_ref[slot * TILES : (slot + 1) * TILES, :] = chosen.astype(BF16)
    row_ref[0:1, :] = ((target & (TILE - 1)) + 1).astype(F32)
    row_ref[1:2, :] = remap_ref[...].reshape(1, TILE)
    row_ref[2:3, :] = jnp.full((1, TILE), share_ref[0], F32)
    row_ref[3:4, :] = jnp.full((1, TILE), share_ref[1], F32)
    row_ref[4:8, :] = jnp.zeros((4, TILE), F32)
    marks = [blocks_ref[at] for at in (4 * odd, 3 - 2 * core, 2, 1 + 2 * core, 4 - 4 * odd)] + [core]
    for at, mark in enumerate(marks):
        mask_ref[at : at + 1, :] = jnp.full((1, 128), mark, jnp.int32).astype(F32)
    mask_ref[6:8, :] = jnp.zeros((2, 128), F32)
    tile = lax.broadcasted_iota(jnp.int32, (1, 128), 1)
    for at, reader in enumerate(
        (place - 2 + 4 * odd, place + 1 - 2 * core, place - 1 + 2 * core, place + 2 - 4 * odd)
    ):
        mask_ref[8 + at : 9 + at, :] = jnp.where(tile == (reader & (TILES - 1)), 1.0, 0.0)
    mask_ref[12:16, :] = jnp.zeros((4, 128), F32)
    tile = lax.broadcasted_iota(jnp.int32, (TILES, 128), 0)
    asked = jnp.zeros((TILES, 128), F32)
    for part in range(OFFSETS):
        if part != REACH:
            reader = (place + part - REACH) & (TILES - 1)
            asked = jnp.where(tile == reader, blocks_ref[part].astype(F32), asked)
    lane = lax.broadcasted_iota(jnp.int32, (TILES, 128), 1)
    asked_ref[...] = jnp.where(lane == ASK_LANE, asked, 0.0)
    for copy in copies[9:]:
        copy.wait()


def interpolate_kernel(
    whole, s0, s1, s2, s3, s4, high_ref, low_ref, factor_ref, row_ref, mask_ref,
    out_ref, neg_ref, pad_ref,
):
    high, low = high_ref[...], low_ref[...]
    second_core = mask_ref[5:6, :] > 0.5
    for n in range(2):
        pieces = []
        for part, source in enumerate((s2, s3, s4, s0, s1) if whole else (s0, s3, s4, s2, s1)):
            if whole and part == 1:
                flat = source.reshape(2 * FULL, BLOCK)
                blocks = [
                    jnp.where(
                        second_core,
                        flat[pl.ds(2 * block + n, LEVELS, stride=4), :],
                        flat[pl.ds(FULL + 2 * block + n, LEVELS, stride=4), :],
                    )
                    for block in range(2)
                ]
                piece = jnp.where(mask_ref[part : part + 1, :] > 0.5, blocks[1], blocks[0])
            elif whole or part == 2:
                flat = (source.at[0] if whole and part == 2 else source).reshape(FULL, BLOCK)
                piece = jnp.where(
                    mask_ref[part : part + 1, :] > 0.5,
                    flat[pl.ds(2 + n, LEVELS, stride=4), :],
                    flat[pl.ds(n, LEVELS, stride=4), :],
                )
            elif part == 1:
                piece = jnp.where(
                    second_core,
                    source[pl.ds(n, LEVELS, stride=2), :],
                    source[pl.ds(HALF + n, LEVELS, stride=2), :],
                )
            else:
                piece = source[pl.ds(n, LEVELS, stride=2), :]
            pieces.append(piece)
        first, second = two_parts(jnp.concatenate(pieces, axis=1))
        pad_ref[n, 0:8, :] = jnp.zeros((8, TILE), F32)
        pad_ref[n, 144:152, :] = jnp.zeros((8, TILE), F32)
        pad_ref[n, 8 : 8 + LEVELS, :] = (
            jnp.dot(second, high, preferred_element_type=F32)
            + jnp.dot(first, low, preferred_element_type=F32)
        ) + jnp.dot(first, high, preferred_element_type=F32)
    total = [jnp.zeros((LEVELS, TILE), F32), jnp.zeros((LEVELS, TILE), F32)]
    for delta in range(-3, 5):
        factor = factor_ref[delta + 3]
        for n in range(2):
            total[n] = total[n] + factor * pad_ref[n, 8 + delta : 8 + delta + LEVELS, :]
    out_ref[0] = total[0]
    out_ref[1] = total[1]
    negative = jnp.minimum(total[0], 0.0) + jnp.minimum(total[1], 0.0)
    share = jnp.broadcast_to(row_ref[2:3, :] + row_ref[3:4, :], (8, TILE))
    for copy in range(4):
        neg_ref[copy, 136:PAD, :] = share
        neg_ref[copy, 0:LEVELS, :] = negative


def send_kernel(mixed_ref, parts_ref, send_ref, row_ref, asked_ref, kept_ref, out_ref, x_ref):
    all_parts = (parts_ref[0] + parts_ref[1]) + (parts_ref[2] + parts_ref[3])
    deficit = all_parts[0:LEVELS, :]
    whole = all_parts[LEVELS : LEVELS + 1, :]
    remap = row_ref[1:2, :]
    x_ref[256:384, :] = jnp.zeros((128, TILE), F32)
    for n in range(2):
        fixed = jnp.maximum(mixed_ref[n], 0.0) + (row_ref[2 + n : 3 + n, :] / whole) * deficit
        kept_ref[n] = (1.0 - remap) * fixed
        moved = remap * fixed
        x_ref[n * 128 : n * 128 + 128, :] = moved[0:128, :]
        x_ref[256 + 16 * n : 256 + 16 * n + 9, :] = moved[128:LEVELS, :]
    x_ref[256 + CELL_LANE : 257 + CELL_LANE, :] = row_ref[0:1, :]
    send = send_ref[...]
    dims = (((1,), (1,)), ((), ()))
    first, second = two_parts(x_ref[...])
    result = lax.dot_general(send, second, dims, preferred_element_type=F32)
    result = result + lax.dot_general(send, first, dims, preferred_element_type=F32)
    rest = asked_ref[...]
    for slot in range(SLOTS):
        rows = result[slot * TILES : (slot + 1) * TILES, :]
        for n in range(2):
            out_ref[pl.ds(2 * slot + n, TILES, stride=ROWS), :] = rows[:, n * 128 : n * 128 + 128]
        tail = rows[:, 256:384]
        if slot:
            tail = pltpu.roll(tail, 32 * slot, axis=1)
        rest = rest + tail
    out_ref[pl.ds(8, TILES, stride=ROWS), :] = rest


def landed(got_ref):
    rest = got_ref[pl.ds(8, TILES, stride=ROWS), :].T
    column = (lax.broadcasted_iota(jnp.int32, (TILE, TILES), 0) + 1).astype(F32)
    sums = [None, None]
    tails = [None, None]
    for slot in range(SLOTS):
        cell = rest[32 * slot + CELL_LANE : 32 * slot + CELL_LANE + 1, :]
        landing = jnp.where(column == cell, 1.0, 0.0).astype(BF16)
        for n in range(2):
            for piece in two_parts(got_ref[pl.ds(2 * slot + n, TILES, stride=ROWS), :]):
                term = jnp.dot(landing, piece, preferred_element_type=F32)
                sums[n] = term if sums[n] is None else sums[n] + term
            tail = rest[32 * slot + 16 * n : 32 * slot + 16 * n + 16, :]
            for piece in two_parts(tail):
                term = lax.dot_general(
                    piece, landing, (((1,), (1,)), ((), ())), preferred_element_type=F32
                )
                tails[n] = term if tails[n] is None else tails[n] + term
    tails = [value[0 : LEVELS - 128, :] for value in tails]
    return [value.T for value in sums], tails, rest[ASK_LANE : ASK_LANE + 1, :]


def land_kernel(kept_ref, got_ref, out_ref):
    sums, tails, _ = landed(got_ref)
    flat = out_ref.reshape(FULL, BLOCK)
    for n in range(2):
        upper = kept_ref[n, 0:128, :] + sums[n]
        lower = kept_ref[n, 128:LEVELS, :] + tails[n]
        for block in range(2):
            lanes = slice(block * BLOCK, (block + 1) * BLOCK)
            flat[pl.ds(2 * block + n, 128, stride=4), :] = upper[:, lanes]
            flat[pl.ds(512 + 2 * block + n, LEVELS - 128, stride=4), :] = lower[:, lanes]


def land_and_select_kernel(
    kept_ref, got_ref, mask_ref, out_ref, behind_ref, pair_ref, across_ref, ahead_ref
):
    sums, tails, asked = landed(got_ref)
    flat = out_ref.reshape(FULL, BLOCK)
    wanted = jnp.sum(mask_ref[8:16, :] * asked, axis=1, keepdims=True)
    asks = [wanted[at : at + 1, :] > 0.5 for at in range(4)]
    for n in range(2):
        for begin, count, values in ((0, 128, sums[n]), (128, LEVELS - 128, tails[n])):
            value = kept_ref[n, begin : begin + count, :] + values
            left, right = value[:, 0:BLOCK], value[:, BLOCK:TILE]
            flat[pl.ds(4 * begin + n, count, stride=4), :] = left
            flat[pl.ds(4 * begin + 2 + n, count, stride=4), :] = right
            for ask, ref in zip(asks, (behind_ref, pair_ref, across_ref, ahead_ref)):
                chosen = jnp.where(ask, right, left)
                ref[pl.ds(2 * begin + n, count, stride=2), :] = chosen
                if ref is pair_ref:
                    ref[pl.ds(HALF + 2 * begin + n, count, stride=2), :] = chosen


def cost(flops, moved):
    return pl.CostEstimate(flops=flops, bytes_accessed=moved, transcendentals=0)


def shards(
    tracers,
    dep_frac,
    vert_frac,
    vert_base,
    dep_blocks,
    dep_slot,
    dep_off,
    remap_share,
    remap_target,
    species_share,
):
    params = pltpu.CompilerParams(vmem_limit_bytes=48 * 1024 * 1024)
    shape = jax.ShapeDtypeStruct
    own = tracers.reshape(2, LEVELS, 2, BLOCK).transpose(1, 2, 0, 3).reshape(LEVELS, 4, BLOCK)
    to_behind, to_across, to_ahead = own, own, own
    high, low, factor, send, row, mask, asked, doubled = pl.pallas_call(
        prepare_kernel,
        name="prepare",
        out_shape=(
            shape((SOURCE, TILE), BF16),
            shape((SOURCE, TILE), BF16),
            shape((8, LEVELS, TILE), F32),
            shape((SLOTS * TILES, TILE), BF16),
            shape((8, TILE), F32),
            shape((16, 128), F32),
            shape((TILES, 128), F32),
            shape((2, LEVELS, 4, BLOCK), F32),
        ),
        in_specs=[pl.BlockSpec(memory_space=pltpu.MemorySpace.HBM)] * 10,
        out_specs=(VMEM,) * 8,
        scratch_shapes=[
            pltpu.VMEM((2, TILE), F32),
            pltpu.VMEM((TILE,), jnp.int32),
            pltpu.VMEM((TILE,), jnp.int32),
            pltpu.VMEM((TILE,), jnp.int32),
            pltpu.VMEM((TILE,), F32),
            pltpu.SMEM((OFFSETS,), jnp.int32),
            pltpu.SMEM((2,), F32),
            pltpu.VMEM((LEVELS, TILE), F32),
            pltpu.VMEM((LEVELS, TILE), jnp.int32),
            pltpu.SemaphoreType.DMA((11,)),
        ],
        compiler_params=params,
        cost_estimate=cost(40_000_000, 2_000_000),
    )(
        *[
            pltpu.with_memory_space_constraint(value, pltpu.MemorySpace.HBM)
            for value in (
                dep_frac, dep_slot, dep_off, remap_target, remap_share, dep_blocks.reshape(OFFSETS),
                species_share, vert_frac, vert_base, own,
            )
        ]
    )

    def interpolate(whole, *sources):
        return pl.pallas_call(
            functools.partial(interpolate_kernel, whole),
            name="interpolate",
            out_shape=(shape((2, LEVELS, TILE), F32), shape((4, PAD, TILE), F32)),
            in_specs=[VMEM] * 10,
            out_specs=(VMEM,) * 2,
            scratch_shapes=[pltpu.VMEM((2, 152, TILE), F32)],
            compiler_params=params,
            cost_estimate=cost(400_000_000, 3_000_000),
        )(*sources, high, low, factor, row, mask)

    dispatch = pl.pallas_call(
        send_kernel,
        name="dispatch",
        out_shape=(shape((2, LEVELS, TILE), F32), shape((TILES * ROWS, 128), F32)),
        in_specs=[VMEM] * 5,
        out_specs=(VMEM,) * 2,
        scratch_shapes=[pltpu.VMEM((384, TILE), F32)],
        compiler_params=params,
        cost_estimate=cost(200_000_000, 2_000_000),
    )
    land = pl.pallas_call(
        land_kernel,
        name="land",
        out_shape=shape((LEVELS, 4, BLOCK), F32),
        in_specs=[VMEM] * 2,
        out_specs=VMEM,
        compiler_params=params,
        cost_estimate=cost(200_000_000, 1_500_000),
    )
    land_and_select = pl.pallas_call(
        land_and_select_kernel,
        name="land_and_select",
        out_shape=(
            shape((LEVELS, 4, BLOCK), F32),
            shape((HALF, 128), F32),
            shape((2 * HALF, 128), F32),
            shape((HALF, 128), F32),
            shape((HALF, 128), F32),
        ),
        in_specs=[VMEM] * 3,
        out_specs=(VMEM,) * 5,
        compiler_params=params,
        cost_estimate=cost(200_000_000, 2_500_000),
    )
    for step_index in range(STEPS):
        behind = swap_chips(to_behind, 1)
        across = swap_across(to_across)
        ahead = swap_chips(to_ahead, 0)
        if step_index == 0:
            pair, own = swap_cores(doubled), doubled
        else:
            pair = swap_cores(to_pair.reshape(2, HALF, BLOCK)).reshape(2 * HALF, BLOCK)
        if step_index == 0:
            mixed, negative = interpolate(True, across, ahead, behind, pair, own)
        else:
            mixed, negative = interpolate(False, behind, ahead, across, pair, own)
        parts = lax.all_to_all(negative, "trc", split_axis=0, concat_axis=0, tiled=True)
        kept, outgoing = dispatch(mixed, parts, send, row, asked)
        arrived = lax.all_to_all(
            outgoing.reshape(TILES, 1, ROWS * 128), "cols", split_axis=0, concat_axis=0, tiled=True
        ).reshape(TILES * ROWS, 128)
        if step_index + 1 < STEPS:
            own, to_behind, to_pair, to_across, to_ahead = land_and_select(kept, arrived, mask)
        else:
            own = land(kept, arrived)
    out = own.reshape(LEVELS, 2, 2, BLOCK).transpose(2, 0, 1, 3)
    return out.reshape(2, LEVELS, TILE)


def solution(mesh):
    return jax.shard_map(
        shards,
        mesh=mesh,
        in_specs=(
            P("trc", None, "cols"),
            P(None, "cols"),
            P(None, "cols"),
            P(None, "cols"),
            P("cols", None, None),
            P("cols"),
            P("cols"),
            P("cols"),
            P("cols"),
            P("trc"),
        ),
        out_specs=P("trc", None, "cols"),
        check_vma=False,
    )
```
